128 devices in a mesh: src: 8 (over z, core), rcv: 16 (over y, x).
Axes of the slice: x: 4, y: 4, z: 4, core: 2. Of those that a mesh axis runs over, the one named last changes fastest.
Arguments:
- data: bfloat16 [2, 16384, 16384], P(None, 'src', 'rcv'), may hold values from -15 to 15
- observed: int32 [256, 256], P('src', 'rcv'), may hold values 0 or 1
- band_width: int32 [1], replicated, may hold values from 24 to 48
- left_factor: float32 [32, 8, 64, 256], P(None, 'src'), may hold values from -1.5 to 1.5
- right_factor: float32 [6, 16, 64, 256], P(None, 'rcv'), may hold values from -1.5 to 1.5
Outputs:
- left_out: float32 [32, 8, 64, 256], P(None, 'src')
- right_out: float32 [6, 16, 64, 256], P(None, 'rcv')
The draws below stay inside these ranges and needn't reach their ends.
All inputs are finite; a program needn't handle non-finite values. No bound on the sum of `observed` on one device may be relied on, other than what follows from the above.
Results may differ from the reference program's by a relative error of at most 0.0044.
The reference program's roundings to bfloat16 on the way count: a program that leaves them out, or rounds other values in their place, can miss the bound.
Values may be sent and summed in bfloat16 or wider, within the bound.
No kernel may reach another device: no remote copies, remote signals or barrier semaphores. Data moves between devices by JAX's collectives and lax.ppermute only.
A program may use at most 128 MiB of HBM per device.

```python
import jax
import jax.numpy as jnp
from jax import lax

BS = 64
NB = 256
K = 128
HB = 96
ITERS = 2
N = 16384
SBLK = 32
TS = 6
N_SRC = 8
N_RCV = 16


def draw_data(key, part):
    key = jax.random.fold_in(key, 11)
    position = jnp.arange(N, dtype=jnp.float32) / (N - 1)
    base = jnp.clip(jax.random.normal(key, (2, N, N), jnp.float32), -5.0, 5.0)
    scale = jnp.exp(jnp.log(3.0) * position)[:, None] * jnp.ones((1, N), jnp.float32)
    return (base * scale[None, :, :]).astype(jnp.bfloat16)


def set_ends(entries, stream_key, low, top_value):
    longest = entries.shape.index(max(entries.shape))
    spots = []
    for shift in (0, 1):
        where = [jax.random.randint(jax.random.fold_in(stream_key, axis), (), 0, length) for axis, length in enumerate(entries.shape)]
        where[longest] = (where[longest] + shift) % entries.shape[longest]
        spots.append(tuple(where))
    return entries.at[spots[0]].set(low).at[spots[1]].set(top_value)


def level_of(stream_key, extent, pieces, least, top_value):
    def one(axis_at, parts):
        steps = jax.random.uniform(jax.random.fold_in(jax.random.fold_in(stream_key, 6), axis_at), (parts,), jnp.float32, least / len(pieces), top_value / len(pieces))
        return jnp.repeat(jnp.exp(steps), extent[axis_at] // parts).reshape((-1,) + (1,) * (len(extent) - axis_at - 1))

    gain = one(*pieces[0])
    for cut in pieces[1:]:
        gain = gain * one(*cut)
    return gain


def gaussian(key, extent, spread, reach, split=(), kind=jnp.bfloat16):
    entries = jax.random.normal(key, extent, jnp.float32) * spread
    if len(split) > 0:
        entries = level_of(key, extent, split, -0.22, 0.18) * entries
    return jnp.clip(entries, min=-reach, max=reach).astype(kind)


def setup_inputs(seed: int = 0) -> dict:
    key_list = jax.random.split(jax.random.key(seed), 6)
    data = draw_data(jax.random.fold_in(key_list[5], 71), 0)
    observed = set_ends((jax.random.randint(key_list[1], (NB, NB), 0, 3) < 2).astype(jnp.int32), jax.random.fold_in(key_list[1], 1), 0, 1)
    band_width = jax.random.randint(key_list[2], (1,), HB // 4, HB // 2 + 1).astype(jnp.int32)
    left_factor = gaussian(key_list[3], (SBLK, N_SRC, BS, 2 * K), 0.25, 1.5, ((1, 8),), jnp.float32)
    right_factor = gaussian(key_list[4], (TS, N_RCV, BS, 2 * K), 0.25, 1.5, ((1, 16),), jnp.float32)
    return {"data": data, "observed": observed, "band_width": band_width, "left_factor": left_factor, "right_factor": right_factor}


epsilon = 1e-6


def stacked(factor):
    half_width = factor.shape[1] // 2
    turned = jnp.concatenate([-factor[:, half_width:], factor[:, :half_width]], axis=1)
    return jnp.concatenate([factor, turned], axis=0)


def times_t(first, second):
    return lax.dot_general(first, second, (((1,), (1,)), ((), ())), preferred_element_type=jnp.float32)


def combine(products):
    count = products.shape[0] // 2
    half_width = products.shape[1] // 2
    upper_part = products[:count]
    lower_part = products[count:]
    return jnp.concatenate([upper_part[:, :half_width] + lower_part[:, half_width:],
                            upper_part[:, half_width:] - lower_part[:, :half_width]], axis=1)


def reference(data, observed, band_width, left_factor, right_factor):
    offsets = jnp.arange(HB, dtype=jnp.int32) - HB // 2
    shifts = offsets // 2
    midpoint_ids = jnp.arange(NB, dtype=jnp.int32)
    source_ids = (midpoint_ids[:, None] - shifts[None, :]) % NB
    receiver_ids = (source_ids + offsets[None, :]) % NB
    blocked = data.reshape(2, NB, BS, NB, BS)
    blocks = blocked[:, source_ids, :, receiver_ids, :]
    target = jnp.transpose(blocks, (0, 3, 2, 1, 4)).reshape(NB * BS, 2 * HB * BS)
    inside = (jnp.abs(offsets) <= band_width[0]).astype(jnp.float32)
    weight = observed[source_ids, receiver_ids].astype(jnp.float32) * inside[None, :]

    def masked(field):
        shaped = field.reshape(NB, BS, 2, HB, BS) * weight[:, None, None, :, None]
        return shaped.reshape(NB * BS, 2 * HB * BS)

    left_full = left_factor.reshape(NB * BS, 2 * K)
    right_full = right_factor.reshape(HB * BS, 2 * K)
    left_b = left_full.astype(jnp.bfloat16)
    right_b = right_full.astype(jnp.bfloat16)
    residual = masked(times_t(left_b, stacked(right_b)) - target.astype(jnp.float32))
    for iteration in range(ITERS):
        residual_b = residual.astype(jnp.bfloat16)
        stacked_right = stacked(right_b)
        gradient = jnp.dot(residual_b, stacked_right, preferred_element_type=jnp.float32)
        curvature = masked(times_t(gradient.astype(jnp.bfloat16), stacked_right))
        step_size = jnp.sum(gradient * gradient) / (jnp.sum(curvature * curvature) + epsilon)
        left_full = left_full - step_size * gradient
        left_b = left_full.astype(jnp.bfloat16)
        residual = residual - step_size * curvature
        residual_b = residual.astype(jnp.bfloat16)
        products = lax.dot_general(residual_b, left_b, (((0,), (0,)), ((), ())), preferred_element_type=jnp.float32)
        gradient_r = combine(products)
        curvature = masked(times_t(left_b, stacked(gradient_r.astype(jnp.bfloat16))))
        step_size = jnp.sum(gradient_r * gradient_r) / (jnp.sum(curvature * curvature) + epsilon)
        right_full = right_full - step_size * gradient_r
        right_b = right_full.astype(jnp.bfloat16)
        residual = residual - step_size * curvature
    return left_full.reshape(left_factor.shape), right_full.reshape(right_factor.shape)
```

```python
import jax
import jax.numpy as jnp
from jax import lax
from jax.experimental import pallas as pl
from jax.experimental.pallas import tpu as pltpu
from jax.sharding import PartitionSpec as P

ITERS = 2
EPSILON = 1e-06
ABSENT = 1024.0
LIMIT = 512.0
VMEM = 56 * 1024 * 1024
CHUNKS = 4
f32 = jnp.float32
bf16 = jnp.bfloat16


def params():
    return pltpu.CompilerParams(vmem_limit_bytes=VMEM)


def whole(shape, **kw):
    return pl.BlockSpec(shape, lambda *_: (0,) * len(shape), **kw)


def nt(a, b):
    return lax.dot_general(a, b, (((1,), (1,)), ((), ())), preferred_element_type=f32)


def nn(a, b):
    return lax.dot_general(a, b, (((1,), (0,)), ((), ())), preferred_element_type=f32)


def tn(a, b):
    return lax.dot_general(a, b, (((0,), (0,)), ((), ())), preferred_element_type=f32)


def store_stacked(factor, out_ref, edge):
    half = factor.shape[1] // 2
    rounded = factor.astype(bf16)
    turned = jnp.concatenate([-rounded[:, half:], rounded[:, :half]], axis=1)
    for t in range(factor.shape[0] // edge):
        rows = slice(t * edge, (t + 1) * edge)
        out_ref[2 * t * edge : (2 * t + 1) * edge, :] = rounded[rows]
        out_ref[(2 * t + 1) * edge : (2 * t + 2) * edge, :] = turned[rows]


def step_of(sums):
    lane = lax.broadcasted_iota(jnp.int32, sums.shape, 1)
    numerator = jnp.sum(jnp.where(lane == 0, sums, 0.0), keepdims=True)
    denominator = jnp.sum(jnp.where(lane == 1, sums, 0.0), keepdims=True)
    return numerator / (denominator + EPSILON)


def weight_rows(w, edge):
    blocks, columns = w.shape
    return jnp.broadcast_to(w[:, None, :], (blocks, edge, columns)).reshape(
        blocks * edge, columns
    )


def pack_kernel(flags_ref, data_ref, out_ref, *, n_src, n_rcv):
    sigma = pl.program_id(0)
    _, groups, _, edge, width = data_ref.shape
    pairs = width // (2 * edge)
    low = lax.broadcasted_iota(jnp.int32, (edge, 2 * edge), 1) < edge
    for u in range(groups):
        for pair in range(pairs):
            re = data_ref[0, u, 0, :, pair * 2 * edge : (pair + 1) * 2 * edge]
            im = data_ref[1, u, 0, :, pair * 2 * edge : (pair + 1) * 2 * edge]
            first = jnp.concatenate([re[:, :edge], im[:, :edge]], axis=1)
            second = jnp.concatenate([re[:, edge:], im[:, edge:]], axis=1)
            for side, block in ((0, first), (1, second)):
                column = 2 * pair + side
                seen = flags_ref[sigma + n_src * u, column] != 0
                rcv = lax.rem(column - sigma - n_src * u + 4 * n_rcv, n_rcv)
                src = lax.rem(sigma + rcv // 2, n_src)
                out_ref[src * n_rcv + rcv, u] = jnp.where(
                    seen, block, jnp.full_like(block, ABSENT)
                )


def first_kernel(meta_ref, blocks_ref, left_ref, right_ref, res_ref, w_ref, grad_ref,
                 stack_ref, acc_ref, *, n_src, n_rcv, slots, edge, per_src, per_rcv):
    chunk = pl.program_id(0)

    @pl.when(chunk == 0)
    def _():
        store_stacked(right_ref[...], stack_ref, edge)

    src = meta_ref[0]
    rcv = meta_ref[1]
    band = meta_ref[2]
    total = n_src * per_src
    mids = left_ref.shape[0] // edge
    groups = per_src // n_src
    sigma = lax.rem(src - rcv // 2 + n_src, n_src)
    kappa = (sigma + rcv // 2 - src) // n_src
    stack = stack_ref[...]
    acc_ref[...] = nt(left_ref[...].astype(bf16), stack)
    for mm in range(mids):
        mid = chunk * mids + mm
        for t in range(slots):
            offset = n_rcv * t + rcv - n_rcv * slots // 2
            inside = jnp.abs(offset) <= band
            v = lax.rem(mid - t + slots // 2 - kappa + 2 * per_src, per_src)
            receiver = lax.rem(sigma + n_src * v + offset + total, total)
            index = ((v // groups) * n_rcv + receiver // per_rcv) * groups + lax.rem(v, groups)
            values = blocks_ref[index].astype(f32)
            keep = jnp.logical_and(values < LIMIT, inside)
            rows = slice(mm * edge, (mm + 1) * edge)
            cols = slice(t * 2 * edge, (t + 1) * 2 * edge)
            res_ref[rows, cols] = jnp.where(keep, acc_ref[rows, cols] - values, 0.0)
            w_ref[mm : mm + 1, cols] = jnp.where(keep[0:1, :], 1.0, 0.0)
    grad_ref[...] = nn(res_ref[...].astype(bf16), stack)


def spread_kernel(parts_ref, out_ref):
    total = jnp.sum(parts_ref[...], axis=0)
    out_ref[...] = jnp.broadcast_to(total[None], out_ref.shape)


def sums_out(numerator, denominator, shape):
    lane = lax.broadcasted_iota(jnp.int32, shape, 1)
    return jnp.where(lane == 0, numerator, jnp.where(lane == 1, denominator, 0.0))


def left_curve_kernel(grad_ref, right_ref, w_ref, out_ref, stack_ref, num_ref, den_ref,
                      *, edge, copies):
    chunk = pl.program_id(0)

    @pl.when(chunk == 0)
    def _():
        store_stacked(right_ref[...], stack_ref, edge)
        num_ref[...] = jnp.zeros_like(num_ref)
        den_ref[...] = jnp.zeros_like(den_ref)

    grad = grad_ref[...]
    curve = nt(grad.astype(bf16), stack_ref[...])
    squares = (curve * curve).reshape(-1, edge, curve.shape[1])
    den_ref[...] += jnp.sum(squares, axis=1) * w_ref[...]
    num_ref[...] += jnp.sum((grad * grad).reshape(-1, 8, grad.shape[1]), axis=0)

    @pl.when(chunk == pl.num_programs(0) - 1)
    def _():
        numerator = jnp.sum(num_ref[...], keepdims=True) * (1.0 / copies)
        denominator = jnp.sum(den_ref[...], keepdims=True)
        out_ref[...] = sums_out(numerator, denominator, out_ref.shape)


def left_update_kernel(sums_ref, grad_ref, left_ref, res_ref, right_ref, w_ref,
                       left_out_ref, *rest, edge, slots, keep_res):
    if keep_res:
        res_out_ref, out_ref, stack_ref, prod_ref = rest
    else:
        out_ref, stack_ref, prod_ref = rest
    chunk = pl.program_id(0)

    @pl.when(chunk == 0)
    def _():
        store_stacked(right_ref[...], stack_ref, edge)
        prod_ref[...] = jnp.zeros_like(prod_ref)

    step = step_of(sums_ref[...])
    grad = grad_ref[...]
    curve = nt(grad.astype(bf16), stack_ref[...])
    left = left_ref[...] - step * grad
    left_out_ref[...] = left
    residual = res_ref[...] - curve * weight_rows(step * w_ref[...], edge)
    if keep_res:
        res_out_ref[...] = residual
    prod_ref[...] += tn(left.astype(bf16), residual.astype(bf16))

    @pl.when(chunk == pl.num_programs(0) - 1)
    def _():
        products = prod_ref[...].T
        half = products.shape[1] // 2
        for t in range(slots):
            upper = products[2 * t * edge : (2 * t + 1) * edge]
            lower = products[(2 * t + 1) * edge : (2 * t + 2) * edge]
            out_ref[t * edge : (t + 1) * edge, :half] = upper[:, :half] + lower[:, half:]
            out_ref[t * edge : (t + 1) * edge, half:] = upper[:, half:] - lower[:, :half]


def right_curve_kernel(grad_ref, left_ref, w_ref, out_ref, stack_ref, den_ref, *, edge, copies):
    chunk = pl.program_id(0)

    @pl.when(chunk == 0)
    def _():
        store_stacked(grad_ref[...], stack_ref, edge)
        den_ref[...] = jnp.zeros_like(den_ref)

    curve = nt(left_ref[...].astype(bf16), stack_ref[...])
    squares = (curve * curve).reshape(-1, edge, curve.shape[1])
    den_ref[...] += jnp.sum(squares, axis=1) * w_ref[...]

    @pl.when(chunk == pl.num_programs(0) - 1)
    def _():
        grad = grad_ref[...]
        numerator = jnp.sum(grad * grad, keepdims=True) * (1.0 / copies)
        denominator = jnp.sum(den_ref[...], keepdims=True)
        out_ref[...] = sums_out(numerator, denominator, out_ref.shape)


def right_update_kernel(sums_ref, grad_r_ref, right_ref, left_ref, res_ref, w_ref,
                        right_out_ref, res_out_ref, grad_ref, stack_ref, turn_ref, *, edge):
    step = step_of(sums_ref[...])

    @pl.when(pl.program_id(0) == 0)
    def _():
        right = right_ref[...] - step * grad_r_ref[...]
        right_out_ref[...] = right
        store_stacked(right, stack_ref, edge)
        store_stacked(grad_r_ref[...], turn_ref, edge)

    curve = nt(left_ref[...].astype(bf16), turn_ref[...])
    residual = res_ref[...] - curve * weight_rows(step * w_ref[...], edge)
    res_out_ref[...] = residual
    grad_ref[...] = nn(residual.astype(bf16), stack_ref[...])


def right_last_kernel(sums_ref, grad_r_ref, right_ref, right_out_ref):
    right_out_ref[...] = right_ref[...] - step_of(sums_ref[...]) * grad_r_ref[...]


def per_device(data, observed, band_width, left_factor, right_factor):
    n_src = lax.axis_size("src")
    n_rcv = lax.axis_size("rcv")
    devices = n_src * n_rcv
    per_src, per_rcv = observed.shape
    edge = data.shape[1] // per_src
    groups = per_src // n_src
    slots = right_factor.shape[0]
    rank2 = left_factor.shape[3]
    rows = per_src * edge
    cols = slots * edge
    step_rows = rows // CHUNKS
    mids = per_src // CHUNKS
    both = ("src", "rcv")

    meta = jnp.concatenate([
        lax.axis_index("src").reshape(1).astype(jnp.int32),
        lax.axis_index("rcv").reshape(1).astype(jnp.int32),
        band_width.astype(jnp.int32),
    ])

    packed = pl.pallas_call(
        lambda *refs: pack_kernel(*refs, n_src=n_src, n_rcv=n_rcv),
        out_shape=jax.ShapeDtypeStruct((devices, groups, edge, 2 * edge), bf16),
        grid_spec=pltpu.PrefetchScalarGridSpec(
            num_scalar_prefetch=1,
            grid=(n_src,),
            in_specs=[
                pl.BlockSpec(
                    (2, groups, 1, edge, data.shape[2]), lambda s, _: (0, 0, s, 0, 0)
                )
            ],
            out_specs=whole((devices, groups, edge, 2 * edge)),
        ),
        compiler_params=params(),
        name="pack",
    )(observed, data.reshape(2, groups, n_src, edge, data.shape[2]))
    arrived = lax.all_to_all(packed, both, split_axis=0, concat_axis=0, tiled=True)
    arrived = arrived.reshape(devices * groups, edge, 2 * edge)

    left = left_factor.reshape(rows, rank2)
    right = right_factor.reshape(cols, rank2)

    def by_chunk(width):
        return pl.BlockSpec((step_rows, width), lambda c, *_: (c, 0))

    w_spec = pl.BlockSpec((mids, 2 * cols), lambda c, *_: (c, 0))
    res_shape = jax.ShapeDtypeStruct((rows, 2 * cols), f32)
    left_shape = jax.ShapeDtypeStruct((rows, rank2), f32)
    right_shape = jax.ShapeDtypeStruct((cols, rank2), f32)
    sums_shape = jax.ShapeDtypeStruct((devices, 128), f32)
    stack_scratch = pltpu.VMEM((2 * cols, rank2), bf16)

    res, weight, parts = pl.pallas_call(
        lambda *refs: first_kernel(
            *refs, n_src=n_src, n_rcv=n_rcv, slots=slots, edge=edge,
            per_src=per_src, per_rcv=per_rcv,
        ),
        out_shape=(res_shape, jax.ShapeDtypeStruct((per_src, 2 * cols), f32), left_shape),
        grid_spec=pltpu.PrefetchScalarGridSpec(
            num_scalar_prefetch=1,
            grid=(CHUNKS,),
            in_specs=[
                whole(arrived.shape, pipeline_mode=pl.Buffered(1)),
                by_chunk(rank2),
                whole((cols, rank2)),
            ],
            out_specs=(by_chunk(2 * cols), w_spec, by_chunk(rank2)),
            scratch_shapes=[stack_scratch, pltpu.VMEM((step_rows, 2 * cols), f32)],
        ),
        compiler_params=params(),
        name="first_gradient",
    )(meta, arrived, left, right)

    def spread(parts, axis, count):
        split = parts.reshape(count, parts.shape[0] // count, rank2)
        landed = lax.all_to_all(split, axis, split_axis=0, concat_axis=0, tiled=True)
        copies = pl.pallas_call(
            spread_kernel,
            out_shape=jax.ShapeDtypeStruct(split.shape, f32),
            compiler_params=params(),
            name="sum_parts",
        )(landed)
        full = lax.all_to_all(copies, axis, split_axis=0, concat_axis=0, tiled=True)
        return full.reshape(parts.shape)

    def shared(sums):
        return lax.all_to_all(sums, both, split_axis=0, concat_axis=0, tiled=True)

    for iteration in range(ITERS):
        last = iteration == ITERS - 1
        grad = spread(parts, "rcv", n_rcv)
        sums = pl.pallas_call(
            lambda *refs: left_curve_kernel(*refs, edge=edge, copies=n_rcv),
            out_shape=sums_shape,
            grid=(CHUNKS,),
            in_specs=[by_chunk(rank2), whole((cols, rank2)), w_spec],
            out_specs=whole((devices, 128)),
            scratch_shapes=[
                stack_scratch,
                pltpu.VMEM((8, rank2), f32),
                pltpu.VMEM((mids, 2 * cols), f32),
            ],
            compiler_params=params(),
            name="left_curve",
        )(grad, right, weight)
        sums = shared(sums)
        outs = pl.pallas_call(
            lambda *refs: left_update_kernel(*refs, edge=edge, slots=slots, keep_res=not last),
            out_shape=(left_shape,) + ((res_shape,) if not last else ()) + (right_shape,),
            grid=(CHUNKS,),
            in_specs=[
                whole((devices, 128)), by_chunk(rank2), by_chunk(rank2), by_chunk(2 * cols),
                whole((cols, rank2)), w_spec,
            ],
            out_specs=(by_chunk(rank2),) + ((by_chunk(2 * cols),) if not last else ())
            + (whole((cols, rank2)),),
            scratch_shapes=[stack_scratch, pltpu.VMEM((rank2, 2 * cols), f32)],
            compiler_params=params(),
            name="left_update",
        )(sums, grad, left, res, right, weight)
        if last:
            left, parts_r = outs
        else:
            left, res, parts_r = outs
        grad_r = spread(parts_r, "src", n_src)
        sums = pl.pallas_call(
            lambda *refs: right_curve_kernel(*refs, edge=edge, copies=n_src),
            out_shape=sums_shape,
            grid=(CHUNKS,),
            in_specs=[whole((cols, rank2)), by_chunk(rank2), w_spec],
            out_specs=whole((devices, 128)),
            scratch_shapes=[stack_scratch, pltpu.VMEM((mids, 2 * cols), f32)],
            compiler_params=params(),
            name="right_curve",
        )(grad_r, left, weight)
        sums = shared(sums)
        if last:
            right = pl.pallas_call(
                right_last_kernel,
                out_shape=right_shape,
                compiler_params=params(),
                name="right_last",
            )(sums, grad_r, right)
        else:
            right, res, parts = pl.pallas_call(
                lambda *refs: right_update_kernel(*refs, edge=edge),
                out_shape=(right_shape, res_shape, left_shape),
                grid=(CHUNKS,),
                in_specs=[
                    whole((devices, 128)), whole((cols, rank2)), whole((cols, rank2)),
                    by_chunk(rank2), by_chunk(2 * cols), w_spec,
                ],
                out_specs=(whole((cols, rank2)), by_chunk(2 * cols), by_chunk(rank2)),
                scratch_shapes=[stack_scratch, stack_scratch],
                compiler_params=params(),
                name="right_update",
            )(sums, grad_r, right, left, res, weight)
    return left.reshape(left_factor.shape), right.reshape(right_factor.shape)


def solution(mesh):
    return jax.shard_map(
        per_device,
        mesh=mesh,
        in_specs=(
            P(None, "src", "rcv"),
            P("src", "rcv"),
            P(),
            P(None, "src", None, None),
            P(None, "rcv", None, None),
        ),
        out_specs=(P(None, "src", None, None), P(None, "rcv", None, None)),
        check_vma=False,
    )
```

```python
import jax
import jax.numpy as jnp
from jax import lax
from jax.experimental import pallas as pl
from jax.experimental.pallas import tpu as pltpu
from jax.sharding import PartitionSpec as P

ITERS = 2
EPSILON = 1e-06
ABSENT = 1024.0
LIMIT = 512.0
VMEM = 56 * 1024 * 1024
CHUNKS = 4
f32 = jnp.float32
bf16 = jnp.bfloat16


def params():
    return pltpu.CompilerParams(vmem_limit_bytes=VMEM)


def whole(shape, **kw):
    return pl.BlockSpec(shape, lambda *_: (0,) * len(shape), **kw)


def nt(a, b):
    return lax.dot_general(a, b, (((1,), (1,)), ((), ())), preferred_element_type=f32)


def nn(a, b):
    return lax.dot_general(a, b, (((1,), (0,)), ((), ())), preferred_element_type=f32)


def tn(a, b):
    return lax.dot_general(a, b, (((0,), (0,)), ((), ())), preferred_element_type=f32)


def store_stacked(factor, out_ref, edge):
    half = factor.shape[1] // 2
    rounded = factor.astype(bf16)
    turned = jnp.concatenate([-rounded[:, half:], rounded[:, :half]], axis=1)
    for t in range(factor.shape[0] // edge):
        rows = slice(t * edge, (t + 1) * edge)
        out_ref[2 * t * edge : (2 * t + 1) * edge, :] = rounded[rows]
        out_ref[(2 * t + 1) * edge : (2 * t + 2) * edge, :] = turned[rows]


def step_of(sums):
    lane = lax.broadcasted_iota(jnp.int32, sums.shape, 1)
    numerator = jnp.sum(jnp.where(lane == 0, sums, 0.0), keepdims=True)
    denominator = jnp.sum(jnp.where(lane == 1, sums, 0.0), keepdims=True)
    return numerator / (denominator + EPSILON)


def weight_rows(w, edge):
    blocks, columns = w.shape
    return jnp.broadcast_to(w[:, None, :], (blocks, edge, columns)).reshape(
        blocks * edge, columns
    )


def pack_kernel(flags_ref, meta_ref, data_ref, out_ref, buf_ref, sem_ref, *, n_src, n_rcv):
    sigma = pl.program_id(0)
    steps = pl.num_programs(0)
    _, groups, _, edge, width = data_ref.shape
    pairs = width // (2 * edge)
    n_pair = n_rcv // 2
    place = lax.rem(sigma, 2)

    def copies(step):
        held = lax.rem(step, 2)
        return [
            pltpu.make_async_copy(
                buf_ref.at[held, q],
                out_ref.at[lax.rem(step + q, n_src) * n_pair + q],
                sem_ref.at[held, q],
            )
            for q in range(n_pair)
        ]

    @pl.when(sigma >= 2)
    def _():
        for copy in copies(sigma - 2):
            copy.wait()

    for u in range(groups):
        for pair in range(pairs):
            re = data_ref[0, u, 0, :, pair * 2 * edge : (pair + 1) * 2 * edge]
            im = data_ref[1, u, 0, :, pair * 2 * edge : (pair + 1) * 2 * edge]
            first = jnp.concatenate([re[:, :edge], im[:, :edge]], axis=1)
            second = jnp.concatenate([re[:, edge:], im[:, edge:]], axis=1)
            for side, block in ((0, first), (1, second)):
                column = 2 * pair + side
                source = sigma + n_src * u
                seen = flags_ref[source, column] != 0
                diff = lax.rem(column - source + 4 * n_rcv, n_rcv)
                q = diff // 2
                turns = (source + diff) // n_rcv + (sigma + q) // n_src
                beta = lax.rem(u + turns + meta_ref[1], 2)
                near = lax.rem(sigma + diff, n_rcv) < n_rcv // 2
                slot = 2 * lax.rem(diff, 2) + jnp.where(near, u // 2, u % 2)
                buf_ref[place, q, beta * groups + slot] = jnp.where(
                    seen, block, jnp.full_like(block, ABSENT)
                )

    for copy in copies(sigma):
        copy.start()

    @pl.when(sigma == steps - 1)
    def _():
        for copy in copies(sigma - 1) + copies(sigma):
            copy.wait()


def first_kernel(meta_ref, blocks_ref, left_ref, right_ref, res_ref, w_ref, grad_ref,
                 stack_ref, acc_ref, *, n_src, n_rcv, slots, edge, per_src, per_rcv):
    chunk = pl.program_id(0)

    @pl.when(chunk == 0)
    def _():
        store_stacked(right_ref[...], stack_ref, edge)

    src = meta_ref[0]
    pair = meta_ref[2]
    beta = meta_ref[3]
    band = meta_ref[4]
    total = n_src * per_src
    mids = left_ref.shape[0]
    rank2 = left_ref.shape[3]
    groups = per_src // n_src
    half = n_rcv // 2
    stack = stack_ref[...]
    acc_ref[...] = nt(left_ref[...].reshape(mids * edge, rank2).astype(bf16), stack)
    for mm in range(mids):
        mid = src + n_src * (2 * (chunk * mids + mm) + beta)
        for column in range(2 * slots):
            tau, t = column // slots, column % slots
            residue = 2 * pair + tau
            offset = n_rcv * t + residue - half * slots
            inside = jnp.abs(offset) <= band
            source = lax.rem(mid - pair - half * t + half * slots // 2 + total, total)
            receiver = lax.rem(source + offset + total, total)
            u = lax.rem(source, per_src) // n_src
            near = lax.rem(lax.rem(source, n_src) + residue, n_rcv) < half
            slot = 2 * tau + jnp.where(near, u // 2, lax.rem(u, 2))
            index = ((source // per_src) * n_rcv + receiver // per_rcv) * groups + slot
            values = blocks_ref[index].astype(f32)
            keep = jnp.logical_and(values < LIMIT, inside)
            rows = slice(mm * edge, (mm + 1) * edge)
            cols = slice(column * 2 * edge, (column + 1) * 2 * edge)
            res_ref[rows, cols] = jnp.where(keep, acc_ref[rows, cols] - values, 0.0)
            w_ref[0, mm : mm + 1, cols] = jnp.where(keep[0:1, :], 1.0, 0.0)
    grad_ref[...] = nn(res_ref[...].astype(bf16), stack)


def spread_kernel(parts_ref, out_ref):
    total = jnp.sum(parts_ref[...], axis=0)
    out_ref[...] = jnp.broadcast_to(total[None], out_ref.shape)


def sums_out(numerator, denominator, shape):
    lane = lax.broadcasted_iota(jnp.int32, shape, 1)
    return jnp.where(lane == 0, numerator, jnp.where(lane == 1, denominator, 0.0))


def left_curve_kernel(grad_ref, right_ref, w_ref, out_ref, stack_ref, num_ref, den_ref,
                      *, edge, copies):
    chunk = pl.program_id(0)

    @pl.when(chunk == 0)
    def _():
        store_stacked(right_ref[...], stack_ref, edge)
        num_ref[...] = jnp.zeros_like(num_ref)
        den_ref[...] = jnp.zeros_like(den_ref)

    grad = grad_ref[...]
    curve = nt(grad.astype(bf16), stack_ref[...])
    squares = (curve * curve).reshape(-1, edge, curve.shape[1])
    den_ref[...] += jnp.sum(squares, axis=1) * w_ref[0]
    num_ref[...] += jnp.sum((grad * grad).reshape(-1, 8, grad.shape[1]), axis=0)

    @pl.when(chunk == pl.num_programs(0) - 1)
    def _():
        numerator = jnp.sum(num_ref[...], keepdims=True) * (1.0 / copies)
        denominator = jnp.sum(den_ref[...], keepdims=True)
        out_ref[...] = sums_out(numerator, denominator, out_ref.shape)


def left_update_kernel(meta_ref, sums_ref, grad_ref, left_ref, res_ref, right_ref, w_ref,
                       left_out_ref, *rest, edge, slots, keep_res):
    if keep_res:
        res_out_ref, out_ref, stack_ref, prod_ref = rest
    else:
        out_ref, stack_ref, prod_ref = rest
    chunk = pl.program_id(0)

    @pl.when(chunk == 0)
    def _():
        store_stacked(right_ref[...], stack_ref, edge)
        prod_ref[...] = jnp.zeros_like(prod_ref)

    step = step_of(sums_ref[...])
    grad = grad_ref[...]
    curve = nt(grad.astype(bf16), stack_ref[...])
    left = left_ref[...].reshape(grad.shape) - step * grad
    left_out_ref[...] = left
    residual = res_ref[...] - curve * weight_rows(step * w_ref[0], edge)
    if keep_res:
        res_out_ref[...] = residual
    prod_ref[...] += tn(left.astype(bf16), residual.astype(bf16))

    @pl.when(chunk == pl.num_programs(0) - 1)
    def _():
        products = prod_ref[...].T
        half = products.shape[1] // 2
        for t in range(slots):
            upper = products[2 * t * edge : (2 * t + 1) * edge]
            lower = products[(2 * t + 1) * edge : (2 * t + 2) * edge]
            out_ref[t * edge : (t + 1) * edge, :half] = upper[:, :half] + lower[:, half:]
            out_ref[t * edge : (t + 1) * edge, half:] = upper[:, half:] - lower[:, :half]


def right_curve_kernel(grad_ref, left_ref, w_ref, out_ref, stack_ref, den_ref, *, edge, copies):
    chunk = pl.program_id(0)

    @pl.when(chunk == 0)
    def _():
        store_stacked(grad_ref[...], stack_ref, edge)
        den_ref[...] = jnp.zeros_like(den_ref)

    curve = nt(left_ref[...].astype(bf16), stack_ref[...])
    squares = (curve * curve).reshape(-1, edge, curve.shape[1])
    den_ref[...] += jnp.sum(squares, axis=1) * w_ref[0]

    @pl.when(chunk == pl.num_programs(0) - 1)
    def _():
        grad = grad_ref[...]
        numerator = jnp.sum(grad * grad, keepdims=True) * (1.0 / copies)
        denominator = jnp.sum(den_ref[...], keepdims=True)
        out_ref[...] = sums_out(numerator, denominator, out_ref.shape)


def right_update_kernel(sums_ref, grad_r_ref, right_ref, left_ref, res_ref, w_ref,
                        right_out_ref, res_out_ref, grad_ref, stack_ref, turn_ref, *, edge):
    step = step_of(sums_ref[...])

    @pl.when(pl.program_id(0) == 0)
    def _():
        right = right_ref[...] - step * grad_r_ref[...]
        right_out_ref[...] = right
        store_stacked(right, stack_ref, edge)
        store_stacked(grad_r_ref[...], turn_ref, edge)

    curve = nt(left_ref[...].astype(bf16), turn_ref[...])
    residual = res_ref[...] - curve * weight_rows(step * w_ref[0], edge)
    res_out_ref[...] = residual
    grad_ref[...] = nn(residual.astype(bf16), stack_ref[...])


def right_last_kernel(meta_ref, sums_ref, grad_r_ref, right_ref, right_out_ref):
    right_out_ref[...] = right_ref[...] - step_of(sums_ref[...]) * grad_r_ref[...]


def per_device(data, observed, band_width, left_factor, right_factor):
    n_src = lax.axis_size("src")
    n_pair = lax.axis_size("pair")
    n_rcv = 2 * n_pair
    devices = n_src * n_rcv
    per_src, per_rcv = observed.shape
    edge = data.shape[1] // per_src
    groups = per_src // n_src
    slots = right_factor.shape[0]
    rank2 = left_factor.shape[3]
    half_mids = per_src // 2
    rows = half_mids * edge
    own_cols = slots * edge
    cols = 2 * own_cols
    step_rows = rows // CHUNKS
    mids = half_mids // CHUNKS
    everyone = ("src", "pair", "beta")
    swap = [(0, 1), (1, 0)]

    src = lax.axis_index("src")
    pair = lax.axis_index("pair")
    beta = lax.axis_index("beta")
    meta = jnp.stack([src, 2 * pair + beta, pair, beta, band_width[0]]).astype(jnp.int32)

    packed = pl.pallas_call(
        lambda *refs: pack_kernel(*refs, n_src=n_src, n_rcv=n_rcv),
        out_shape=jax.ShapeDtypeStruct((n_src * n_pair, 2 * groups, edge, 2 * edge), bf16),
        grid_spec=pltpu.PrefetchScalarGridSpec(
            num_scalar_prefetch=2,
            grid=(n_src,),
            in_specs=[
                pl.BlockSpec((2, groups, 1, edge, data.shape[2]), lambda s, *_: (0, 0, s, 0, 0))
            ],
            out_specs=pl.BlockSpec(memory_space=pl.ANY),
            scratch_shapes=[
                pltpu.VMEM((2, n_pair, 2 * groups, edge, 2 * edge), bf16),
                pltpu.SemaphoreType.DMA((2, n_pair)),
            ],
        ),
        compiler_params=params(),
        name="pack",
    )(observed, meta, data.reshape(2, groups, n_src, edge, data.shape[2]))
    packed = packed.reshape(devices, groups, edge, 2 * edge)
    arrived = lax.all_to_all(packed, everyone, split_axis=0, concat_axis=0, tiled=True)
    arrived = arrived.reshape(devices * groups, edge, 2 * edge)

    left = left_factor.reshape(half_mids, 2, edge, rank2)
    own_right = right_factor.reshape(own_cols, rank2)
    other_right = lax.ppermute(own_right, "beta", swap)
    right = jnp.concatenate([
        jnp.where(beta == 0, own_right, other_right),
        jnp.where(beta == 0, other_right, own_right),
    ])

    def by_chunk(width):
        return pl.BlockSpec((step_rows, width), lambda c, *_: (c, 0))

    w_spec = pl.BlockSpec((1, mids, 2 * cols), lambda c, *_: (c, 0, 0))
    res_shape = jax.ShapeDtypeStruct((rows, 2 * cols), f32)
    left_shape = jax.ShapeDtypeStruct((rows, rank2), f32)
    right_shape = jax.ShapeDtypeStruct((cols, rank2), f32)
    sums_shape = jax.ShapeDtypeStruct((devices, 128), f32)
    stack_scratch = pltpu.VMEM((2 * cols, rank2), bf16)

    res, weight, parts = pl.pallas_call(
        lambda *refs: first_kernel(
            *refs, n_src=n_src, n_rcv=n_rcv, slots=slots, edge=edge,
            per_src=per_src, per_rcv=per_rcv,
        ),
        out_shape=(
            res_shape, jax.ShapeDtypeStruct((CHUNKS, mids, 2 * cols), f32), left_shape
        ),
        grid_spec=pltpu.PrefetchScalarGridSpec(
            num_scalar_prefetch=1,
            grid=(CHUNKS,),
            in_specs=[
                whole(arrived.shape, pipeline_mode=pl.Buffered(1)),
                pl.BlockSpec((mids, 1, edge, rank2), lambda c, meta_ref: (c, meta_ref[3], 0, 0)),
                whole((cols, rank2)),
            ],
            out_specs=(by_chunk(2 * cols), w_spec, by_chunk(rank2)),
            scratch_shapes=[stack_scratch, pltpu.VMEM((step_rows, 2 * cols), f32)],
        ),
        compiler_params=params(),
        name="first_gradient",
    )(meta, arrived, left, right)

    def spread(parts, axis, count):
        split = parts.reshape(count, parts.shape[0] // count, rank2)
        landed = lax.all_to_all(split, axis, split_axis=0, concat_axis=0, tiled=True)
        copies = pl.pallas_call(
            spread_kernel,
            out_shape=jax.ShapeDtypeStruct(split.shape, f32),
            compiler_params=params(),
            name="sum_parts",
        )(landed)
        full = lax.all_to_all(copies, axis, split_axis=0, concat_axis=0, tiled=True)
        return full.reshape(parts.shape)

    def shared(sums):
        return lax.all_to_all(sums, everyone, split_axis=0, concat_axis=0, tiled=True)

    for iteration in range(ITERS):
        last = iteration == ITERS - 1
        grad = spread(parts, "pair", n_pair)
        sums = pl.pallas_call(
            lambda *refs: left_curve_kernel(*refs, edge=edge, copies=n_pair),
            out_shape=sums_shape,
            grid=(CHUNKS,),
            in_specs=[by_chunk(rank2), whole((cols, rank2)), w_spec],
            out_specs=whole((devices, 128)),
            scratch_shapes=[
                stack_scratch,
                pltpu.VMEM((8, rank2), f32),
                pltpu.VMEM((mids, 2 * cols), f32),
            ],
            compiler_params=params(),
            name="left_curve",
        )(grad, right, weight)
        sums = shared(sums)
        own_left = (
            pl.BlockSpec((mids, 1, edge, rank2), lambda c, meta_ref: (c, meta_ref[3], 0, 0))
            if iteration == 0 else by_chunk(rank2)
        )
        outs = pl.pallas_call(
            lambda *refs: left_update_kernel(*refs, edge=edge, slots=2 * slots, keep_res=not last),
            out_shape=(left_shape,) + ((res_shape,) if not last else ()) + (right_shape,),
            grid_spec=pltpu.PrefetchScalarGridSpec(
                num_scalar_prefetch=1,
                grid=(CHUNKS,),
                in_specs=[
                    whole((devices, 128)), by_chunk(rank2), own_left, by_chunk(2 * cols),
                    whole((cols, rank2)), w_spec,
                ],
                out_specs=(by_chunk(rank2),) + ((by_chunk(2 * cols),) if not last else ())
                + (whole((cols, rank2)),),
                scratch_shapes=[stack_scratch, pltpu.VMEM((rank2, 2 * cols), f32)],
            ),
            compiler_params=params(),
            name="left_update",
        )(meta, sums, grad, left, res, right, weight)
        if last:
            left, parts_r = outs
            other_left = lax.ppermute(left, "beta", swap)
        else:
            left, res, parts_r = outs
        grad_r = spread(parts_r, ("src", "beta"), 2 * n_src)
        sums = pl.pallas_call(
            lambda *refs: right_curve_kernel(*refs, edge=edge, copies=2 * n_src),
            out_shape=sums_shape,
            grid=(CHUNKS,),
            in_specs=[whole((cols, rank2)), by_chunk(rank2), w_spec],
            out_specs=whole((devices, 128)),
            scratch_shapes=[stack_scratch, pltpu.VMEM((mids, 2 * cols), f32)],
            compiler_params=params(),
            name="right_curve",
        )(grad_r, left, weight)
        sums = shared(sums)
        if last:
            own = pl.BlockSpec((own_cols, rank2), lambda c, meta_ref: (meta_ref[3], 0))
            right = pl.pallas_call(
                right_last_kernel,
                out_shape=jax.ShapeDtypeStruct((own_cols, rank2), f32),
                grid_spec=pltpu.PrefetchScalarGridSpec(
                    num_scalar_prefetch=1,
                    grid=(1,),
                    in_specs=[whole((devices, 128)), own, own],
                    out_specs=whole((own_cols, rank2)),
                ),
                compiler_params=params(),
                name="right_last",
            )(meta, sums, grad_r, right)
        else:
            right, res, parts = pl.pallas_call(
                lambda *refs: right_update_kernel(*refs, edge=edge),
                out_shape=(right_shape, res_shape, left_shape),
                grid=(CHUNKS,),
                in_specs=[
                    whole((devices, 128)), whole((cols, rank2)), whole((cols, rank2)),
                    by_chunk(rank2), by_chunk(2 * cols), w_spec,
                ],
                out_specs=(whole((cols, rank2)), by_chunk(2 * cols), by_chunk(rank2)),
                scratch_shapes=[stack_scratch, stack_scratch],
                compiler_params=params(),
                name="right_update",
            )(sums, grad_r, right, left, res, weight)
    own_left = left.reshape(half_mids, 1, edge, rank2)
    other_left = other_left.reshape(half_mids, 1, edge, rank2)
    parity = lax.broadcasted_iota(jnp.int32, (half_mids, 2, edge, rank2), 1)
    left = jnp.where(parity == beta, own_left, other_left)
    return left.reshape(left_factor.shape), right.reshape(right_factor.shape)


def solution(mesh):
    n_src, n_rcv = mesh.shape["src"], mesh.shape["rcv"]
    split = jax.sharding.Mesh(
        mesh.devices.reshape(n_src, n_rcv // 2, 2), ("src", "pair", "beta")
    )
    rcv = ("pair", "beta")
    return jax.shard_map(
        per_device,
        mesh=split,
        in_specs=(
            P(None, "src", rcv),
            P("src", rcv),
            P(),
            P(None, "src", None, None),
            P(None, rcv, None, None),
        ),
        out_specs=(P(None, "src", None, None), P(None, rcv, None, None)),
        check_vma=False,
    )
```

```python
import jax
import jax.numpy as jnp
from jax import lax
from jax.experimental import pallas as pl
from jax.experimental.pallas import tpu as pltpu
from jax.sharding import PartitionSpec as P

ITERS = 2
EPSILON = 1e-06
ABSENT = 1024.0
LIMIT = 512.0
VMEM = 40 * 1024 * 1024
f32 = jnp.float32
bf16 = jnp.bfloat16


def params():
    return pltpu.CompilerParams(vmem_limit_bytes=VMEM)


def whole(shape):
    return pl.BlockSpec(shape, lambda *_: (0,) * len(shape))


def mod(x, n):
    assert n & (n - 1) == 0
    return x & (n - 1)


def div(x, n):
    assert n & (n - 1) == 0
    return x >> (n.bit_length() - 1)


def nt(a, b):
    return lax.dot_general(a, b, (((1,), (1,)), ((), ())), preferred_element_type=f32)


def nn(a, b):
    return lax.dot_general(a, b, (((1,), (0,)), ((), ())), preferred_element_type=f32)


def tn(a, b):
    return lax.dot_general(a, b, (((0,), (0,)), ((), ())), preferred_element_type=f32)


def stacked(factor, edge):
    half = factor.shape[1] // 2
    rounded = factor.astype(bf16)
    turned = jnp.concatenate([-rounded[:, half:], rounded[:, :half]], axis=1)
    pieces = []
    for t in range(factor.shape[0] // edge):
        rows = slice(t * edge, (t + 1) * edge)
        pieces += [rounded[rows], turned[rows]]
    return jnp.concatenate(pieces, axis=0)


def combined(products, edge):
    half = products.shape[1] // 2
    pieces = []
    for t in range(products.shape[0] // (2 * edge)):
        upper = products[2 * t * edge : (2 * t + 1) * edge]
        lower = products[(2 * t + 1) * edge : (2 * t + 2) * edge]
        pieces.append(jnp.concatenate(
            [upper[:, :half] + lower[:, half:], upper[:, half:] - lower[:, :half]], axis=1
        ))
    return jnp.concatenate(pieces, axis=0)


def step_of(sums):
    lane = lax.broadcasted_iota(jnp.int32, sums.shape, 1)
    numerator = jnp.sum(jnp.where(lane == 0, sums, 0.0), keepdims=True)
    denominator = jnp.sum(jnp.where(lane == 1, sums, 0.0), keepdims=True)
    return numerator / (denominator + EPSILON)


def sums_out(numerator, denominator, shape):
    lane = lax.broadcasted_iota(jnp.int32, shape, 1)
    return jnp.where(lane == 0, numerator, jnp.where(lane == 1, denominator, 0.0))


def weighted(field, weight, edge):
    blocks, columns = weight.shape
    return (field.reshape(blocks, edge, columns) * weight[:, None, :]).reshape(field.shape)


def pack_kernel(flags_ref, meta_ref, data_ref, out_ref, buf_ref, sem_ref, *, n_src, n_rcv):
    sigma = pl.program_id(0)
    steps = pl.num_programs(0)
    _, groups, _, edge, width = data_ref.shape
    pairs = width // (2 * edge)
    n_pair = n_rcv // 2
    place = mod(sigma, 2)

    def copies(step):
        held = mod(step, 2)
        return [
            pltpu.make_async_copy(
                buf_ref.at[held, q],
                out_ref.at[mod(step + q, n_src) * n_pair + q],
                sem_ref.at[held, q],
            )
            for q in range(n_pair)
        ]

    @pl.when(sigma >= 2)
    def _():
        for copy in copies(sigma - 2):
            copy.wait()

    for u in range(groups):
        for pair in range(pairs):
            re = data_ref[0, u, 0, :, pair * 2 * edge : (pair + 1) * 2 * edge]
            im = data_ref[1, u, 0, :, pair * 2 * edge : (pair + 1) * 2 * edge]
            first = jnp.concatenate([re[:, :edge], im[:, :edge]], axis=1)
            second = jnp.concatenate([re[:, edge:], im[:, edge:]], axis=1)
            for side, block in ((0, first), (1, second)):
                column = 2 * pair + side
                source = sigma + n_src * u
                seen = flags_ref[source, column] != 0
                diff = mod(column - source, n_rcv)
                q = div(diff, 2)
                turns = div(source + diff, n_rcv) + div(sigma + q, n_src)
                beta = mod(u + turns + meta_ref[1], 2)
                near = mod(sigma + diff, n_rcv) < n_rcv // 2
                slot = 2 * mod(diff, 2) + jnp.where(near, u // 2, u % 2)
                buf_ref[place, q, beta * groups + slot] = jnp.where(
                    seen, block, jnp.full_like(block, ABSENT)
                )

    for copy in copies(sigma):
        copy.start()

    @pl.when(sigma == steps - 1)
    def _():
        for copy in copies(sigma - 1) + copies(sigma):
            copy.wait()


def first_kernel(meta_ref, blocks_ref, left_ref, right_ref, target_ref, w_ref, grad_ref,
                 held_ref, sem_ref, left_b_ref, *, n_src, n_rcv, slots, edge, per_src, per_rcv):
    step = pl.program_id(0)
    steps = pl.num_programs(0)
    src, pair, beta, band = meta_ref[0], meta_ref[2], meta_ref[3], meta_ref[4]
    total = n_src * per_src
    mids = left_ref.shape[0]
    groups = per_src // n_src
    half = n_rcv // 2
    width = 2 * edge
    per_step = target_ref.shape[2] // width

    def offset_of(column):
        tau = jnp.where(column >= slots, 1, 0)
        return n_rcv * (column - slots * tau) + 2 * pair + tau - half * slots, tau

    def copies(at):
        held = mod(at, 2)
        found = []
        for side in range(per_step):
            offset, tau = offset_of(at * per_step + side)
            residue = 2 * pair + tau
            for mm in range(mids):
                mid = src + n_src * (2 * mm + beta)
                source = mod(mid - (offset >> 1), total)
                receiver = mod(source + offset, total)
                u = div(mod(source, per_src), n_src)
                near = mod(mod(source, n_src) + residue, n_rcv) < half
                slot = 2 * tau + jnp.where(near, div(u, 2), mod(u, 2))
                index = (div(source, per_src) * n_rcv + div(receiver, per_rcv)) * groups + slot
                found.append(pltpu.make_async_copy(
                    blocks_ref.at[index],
                    held_ref.at[held, side, pl.ds(mm * edge, edge)],
                    sem_ref.at[held, side, mm],
                ))
        return found

    @pl.when(step == 0)
    def _():
        for copy in copies(step):
            copy.start()
        left_b_ref[...] = left_ref[...].reshape(left_b_ref.shape).astype(bf16)
        grad_ref[...] = jnp.zeros_like(grad_ref)

    @pl.when(step + 1 < steps)
    def _():
        for copy in copies(step + 1):
            copy.start()

    stack = stacked(right_ref[...], edge)
    product = nt(left_b_ref[...], stack)
    for copy in copies(step):
        copy.wait()
    pieces = []
    for side in range(per_step):
        offset, _ = offset_of(step * per_step + side)
        inside = jnp.abs(offset) <= band
        cols = slice(side * width, (side + 1) * width)
        values = held_ref[mod(step, 2), side]
        wide = values.astype(f32)
        keep = jnp.logical_and(wide < LIMIT, inside)
        target_ref[0, :, cols] = jnp.where(keep, wide, 0.0).astype(bf16)
        for mm in range(mids):
            w_ref[0, mm : mm + 1, cols] = jnp.where(keep[mm * edge : mm * edge + 1], 1.0, 0.0)
        pieces.append(jnp.where(keep, product[:, cols] - wide, 0.0).astype(bf16))
    grad_ref[...] += nn(jnp.concatenate(pieces, axis=1), stack)


def spread_kernel(parts_ref, out_ref):
    total = jnp.sum(parts_ref[...], axis=0)
    out_ref[...] = jnp.broadcast_to(total[None], out_ref.shape)


def curve_kernel(left_ref, right_ref, w_ref, out_ref, *, edge, copies, by_left):
    left = left_ref[...]
    left_b = left.astype(bf16)
    mids = left.shape[0] // edge
    tiles, _, width = w_ref.shape
    rows = width // 2
    total = jnp.zeros((mids, width), f32)
    for tile in range(tiles):
        curve = nt(left_b, stacked(right_ref[tile * rows : (tile + 1) * rows, :], edge))
        squares = (curve * curve).reshape(mids, edge, width)
        total = total + jnp.sum(squares, axis=1) * w_ref[tile]
    grad = left if by_left else right_ref[...]
    numerator = jnp.sum(grad * grad, keepdims=True) * (1.0 / copies)
    out_ref[...] = sums_out(numerator, jnp.sum(total, keepdims=True), out_ref.shape)


def residual_of(target_ref, w_ref, lefts, stacks, steps, edge):
    residual = nt(lefts[0], stacks[0]) - target_ref[0].astype(f32)
    for left, stack, step in zip(lefts[1:], stacks[1:], steps):
        residual = residual - step * nt(left, stack)
    return weighted(residual, w_ref[0], edge).astype(bf16)


def left_update_kernel(meta_ref, *refs, edge, updates):
    taken = iter(refs)
    sums = [next(taken) for _ in range(updates)]
    target_ref, w_ref = next(taken), next(taken)
    start_ref = next(taken)
    first_grad_ref = next(taken)
    right_ref = next(taken)
    if updates == 3:
        left_ref, grad_ref = next(taken), next(taken)
        grad_r_ref, right_now_ref = next(taken), next(taken)
    left_out_ref, out_ref = next(taken), next(taken)
    held = list(taken)
    steps = [step_of(ref[...]) for ref in sums]

    @pl.when(pl.program_id(0) == 0)
    def _():
        start = start_ref[...].reshape(left_out_ref.shape)
        held[0][...] = start.astype(bf16)
        held[1][...] = first_grad_ref[...].astype(bf16)
        if updates == 1:
            new = start - steps[0] * first_grad_ref[...]
            held[2][...] = new.astype(bf16)
        else:
            held[2][...] = left_ref[...].astype(bf16)
            held[3][...] = grad_ref[...].astype(bf16)
            new = left_ref[...] - steps[2] * grad_ref[...]
            held[4][...] = new.astype(bf16)
        left_out_ref[...] = new

    stack = stacked(right_ref[...], edge)
    stacks = [stack, stack]
    lefts = [held[0][...], held[1][...]]
    if updates == 3:
        stacks += [stacked(grad_r_ref[...], edge), stacked(right_now_ref[...], edge)]
        lefts += [held[2][...], held[3][...]]
    residual = residual_of(target_ref, w_ref, lefts, stacks, steps, edge)
    out_ref[...] = combined(tn(held[-1][...], residual).T, edge)


def right_update_kernel(meta_ref, sums_ref, sums_r_ref, target_ref, w_ref, start_ref,
                        first_grad_ref, right_ref, left_ref, grad_r_ref,
                        right_out_ref, grad_ref, *held, edge):
    step = step_of(sums_ref[...])
    step_r = step_of(sums_r_ref[...])

    @pl.when(pl.program_id(0) == 0)
    def _():
        held[0][...] = start_ref[...].reshape(left_ref.shape).astype(bf16)
        held[1][...] = first_grad_ref[...].astype(bf16)
        held[2][...] = left_ref[...].astype(bf16)
        grad_ref[...] = jnp.zeros_like(grad_ref)

    right = right_ref[...] - step_r * grad_r_ref[...]
    right_out_ref[...] = right
    stack = stacked(right_ref[...], edge)
    residual = residual_of(
        target_ref, w_ref, [ref[...] for ref in held],
        [stack, stack, stacked(grad_r_ref[...], edge)], [step, step_r], edge,
    )
    grad_ref[...] += nn(residual, stacked(right, edge))


def right_last_kernel(meta_ref, sums_ref, grad_r_ref, right_ref, right_out_ref):
    right_out_ref[...] = right_ref[...] - step_of(sums_ref[...]) * grad_r_ref[...]


def per_device(data, observed, band_width, left_factor, right_factor):
    n_src = lax.axis_size("src")
    n_pair = lax.axis_size("pair")
    n_rcv = 2 * n_pair
    devices = n_src * n_rcv
    per_src, per_rcv = observed.shape
    edge = data.shape[1] // per_src
    groups = per_src // n_src
    slots = right_factor.shape[0]
    rank2 = left_factor.shape[3]
    mids = per_src // 2
    rows = mids * edge
    own_cols = slots * edge
    cols = 2 * own_cols
    width = 4 * edge
    tiles = 2 * cols // width
    everyone = ("src", "pair", "beta")
    swap = [(0, 1), (1, 0)]

    src = lax.axis_index("src")
    pair = lax.axis_index("pair")
    beta = lax.axis_index("beta")
    meta = jnp.stack([src, 2 * pair + beta, pair, beta, band_width[0]]).astype(jnp.int32)

    own_right = right_factor.reshape(own_cols, rank2)
    other_right = lax.ppermute(own_right, "beta", swap)
    packed = pl.pallas_call(
        lambda *refs: pack_kernel(*refs, n_src=n_src, n_rcv=n_rcv),
        out_shape=jax.ShapeDtypeStruct((n_src * n_pair, 2 * groups, edge, 2 * edge), bf16),
        grid_spec=pltpu.PrefetchScalarGridSpec(
            num_scalar_prefetch=2,
            grid=(n_src,),
            in_specs=[
                pl.BlockSpec((2, groups, 1, edge, data.shape[2]), lambda s, *_: (0, 0, s, 0, 0))
            ],
            out_specs=pl.BlockSpec(memory_space=pl.ANY),
            scratch_shapes=[
                pltpu.VMEM((2, n_pair, 2 * groups, edge, 2 * edge), bf16),
                pltpu.SemaphoreType.DMA((2, n_pair)),
            ],
        ),
        compiler_params=params(),
        name="pack",
    )(observed, meta, data.reshape(2, groups, n_src, edge, data.shape[2]))
    right = jnp.concatenate([
        jnp.where(beta == 0, own_right, other_right),
        jnp.where(beta == 0, other_right, own_right),
    ])
    packed, right = lax.optimization_barrier((packed, right))
    packed = packed.reshape(devices, groups, edge, 2 * edge)
    arrived = lax.all_to_all(packed, everyone, split_axis=0, concat_axis=0, tiled=True)
    arrived = arrived.reshape(devices * groups, edge, 2 * edge)

    start = left_factor.reshape(mids, 2, edge, rank2)

    start_spec = pl.BlockSpec((mids, 1, edge, rank2), lambda c, meta_ref: (0, meta_ref[3], 0, 0))
    left_spec = whole((rows, rank2))
    right_spec = pl.BlockSpec((width // 2, rank2), lambda c, *_: (c, 0))
    target_spec = pl.BlockSpec((1, rows, width), lambda c, *_: (c, 0, 0))
    w_spec = pl.BlockSpec((1, mids, width), lambda c, *_: (c, 0, 0))
    sums_spec = whole((devices, 128))
    left_shape = jax.ShapeDtypeStruct((rows, rank2), f32)
    right_shape = jax.ShapeDtypeStruct((cols, rank2), f32)
    sums_shape = jax.ShapeDtypeStruct((devices, 128), f32)
    left_scratch = pltpu.VMEM((rows, rank2), bf16)

    def call(kernel, name, out_shape, in_specs, out_specs, scratch=(), grid=(tiles,)):
        return pl.pallas_call(
            kernel,
            out_shape=out_shape,
            grid_spec=pltpu.PrefetchScalarGridSpec(
                num_scalar_prefetch=1,
                grid=grid,
                in_specs=in_specs,
                out_specs=out_specs,
                scratch_shapes=list(scratch),
            ),
            compiler_params=params(),
            name=name,
        )

    target, weight, parts = call(
        lambda *refs: first_kernel(
            *refs, n_src=n_src, n_rcv=n_rcv, slots=slots, edge=edge,
            per_src=per_src, per_rcv=per_rcv,
        ),
        "first_gradient",
        (
            jax.ShapeDtypeStruct((tiles, rows, width), bf16),
            jax.ShapeDtypeStruct((tiles, mids, width), f32),
            left_shape,
        ),
        [pl.BlockSpec(memory_space=pl.ANY), start_spec, right_spec],
        (target_spec, w_spec, left_spec),
        [
            pltpu.VMEM((2, width // (2 * edge), rows, 2 * edge), bf16),
            pltpu.SemaphoreType.DMA((2, width // (2 * edge), mids)),
            left_scratch,
        ],
    )(meta, arrived, start, right)

    def spread(parts, axis, count):
        split = parts.reshape(count, parts.shape[0] // count, rank2)
        landed = lax.all_to_all(split, axis, split_axis=0, concat_axis=0, tiled=True)
        copies = pl.pallas_call(
            spread_kernel,
            out_shape=jax.ShapeDtypeStruct(split.shape, f32),
            compiler_params=params(),
            name="sum_parts",
        )(landed)
        full = lax.all_to_all(copies, axis, split_axis=0, concat_axis=0, tiled=True)
        return full.reshape(parts.shape)

    def shared(left, right, by_left, copies):
        sums = pl.pallas_call(
            lambda *refs: curve_kernel(*refs, edge=edge, copies=copies, by_left=by_left),
            out_shape=sums_shape,
            compiler_params=params(),
            name="left_curve" if by_left else "right_curve",
        )(left, right, weight)
        return lax.all_to_all(sums, everyone, split_axis=0, concat_axis=0, tiled=True)

    lefts, grads, rights, grads_r, sums = [start], [], [right], [], []
    for iteration in range(ITERS):
        grad = spread(parts, "pair", n_pair)
        grads.append(grad)
        sums.append(shared(grad, rights[-1], True, n_pair))
        updates = 2 * iteration + 1
        more = updates == 3
        left, parts_r = call(
            lambda *refs: left_update_kernel(*refs, edge=edge, updates=updates),
            "left_update",
            (left_shape, right_shape),
            [sums_spec] * updates
            + [target_spec, w_spec, start_spec, left_spec, right_spec]
            + ([left_spec, left_spec, right_spec, right_spec] if more else []),
            (left_spec, right_spec),
            [left_scratch] * (updates + 2),
        )(
            meta, *sums, target, weight, start, grads[0], rights[0],
            *([lefts[1], grads[1], grads_r[0], rights[1]] if more else []),
        )
        lefts.append(left)
        if more:
            other_left = lax.ppermute(left, "beta", swap)
        grad_r = spread(parts_r, ("src", "beta"), 2 * n_src)
        grads_r.append(grad_r)
        sums.append(shared(left, grad_r, False, 2 * n_src))
        if more:
            own = pl.BlockSpec((own_cols, rank2), lambda c, meta_ref: (meta_ref[3], 0))
            right_out = call(
                right_last_kernel,
                "right_last",
                jax.ShapeDtypeStruct((own_cols, rank2), f32),
                [sums_spec, own, own],
                whole((own_cols, rank2)),
                grid=(1,),
            )(meta, sums[-1], grad_r, rights[-1])
        else:
            right, parts = call(
                lambda *refs: right_update_kernel(*refs, edge=edge),
                "right_update",
                (right_shape, left_shape),
                [sums_spec, sums_spec, target_spec, w_spec, start_spec, left_spec,
                 right_spec, left_spec, right_spec],
                (right_spec, left_spec),
                [left_scratch] * 3,
            )(meta, *sums, target, weight, start, grads[0], rights[0], left, grad_r)
            rights.append(right)
    own_left = lefts[-1].reshape(mids, 1, edge, rank2)
    other_left = other_left.reshape(mids, 1, edge, rank2)
    parity = lax.broadcasted_iota(jnp.int32, (mids, 2, edge, rank2), 1)
    left_out = jnp.where(parity == beta, own_left, other_left)
    return left_out.reshape(left_factor.shape), right_out.reshape(right_factor.shape)


def solution(mesh):
    n_src, n_rcv = mesh.shape["src"], mesh.shape["rcv"]
    split = jax.sharding.Mesh(
        mesh.devices.reshape(n_src, n_rcv // 2, 2), ("src", "pair", "beta")
    )
    rcv = ("pair", "beta")
    return jax.shard_map(
        per_device,
        mesh=split,
        in_specs=(
            P(None, "src", rcv),
            P("src", rcv),
            P(),
            P(None, "src", None, None),
            P(None, rcv, None, None),
        ),
        out_specs=(P(None, "src", None, None), P(None, rcv, None, None)),
        check_vma=False,
    )
```

```python
import jax
import jax.numpy as jnp
from jax import lax
from jax.experimental import pallas as pl
from jax.experimental.pallas import tpu as pltpu
from jax.sharding import PartitionSpec as P

RING = 4
EPSILON = 1e-06
ABSENT = 1024.0
LIMIT = 512.0
VMEM = 24 * 1024 * 1024
f32 = jnp.float32
bf16 = jnp.bfloat16


def params():
    return pltpu.CompilerParams(vmem_limit_bytes=VMEM)


def whole(shape):
    return pl.BlockSpec(shape, lambda *_: (0,) * len(shape))


def mod(x, n):
    assert n & (n - 1) == 0
    return x & (n - 1)


def div(x, n):
    assert n & (n - 1) == 0
    return x >> (n.bit_length() - 1)


def nt(a, b):
    return lax.dot_general(a, b, (((1,), (1,)), ((), ())), preferred_element_type=f32)


def nn(a, b):
    return lax.dot_general(a, b, (((1,), (0,)), ((), ())), preferred_element_type=f32)


def tn(a, b):
    return lax.dot_general(a, b, (((0,), (0,)), ((), ())), preferred_element_type=f32)


def stacked(factor, edge):
    half = factor.shape[1] // 2
    rounded = factor.astype(bf16)
    turned = jnp.concatenate([-rounded[:, half:], rounded[:, :half]], axis=1)
    pieces = []
    for t in range(factor.shape[0] // edge):
        rows = slice(t * edge, (t + 1) * edge)
        pieces += [rounded[rows], turned[rows]]
    return jnp.concatenate(pieces, axis=0)


def combined(products, edge):
    half = products.shape[1] // 2
    pieces = []
    for t in range(products.shape[0] // (2 * edge)):
        upper = products[2 * t * edge : (2 * t + 1) * edge]
        lower = products[(2 * t + 1) * edge : (2 * t + 2) * edge]
        pieces.append(jnp.concatenate(
            [upper[:, :half] + lower[:, half:], upper[:, half:] - lower[:, :half]], axis=1
        ))
    return jnp.concatenate(pieces, axis=0)


def step_of(sums):
    lane = lax.broadcasted_iota(jnp.int32, sums.shape, 1)
    numerator = jnp.sum(jnp.where(lane == 0, sums, 0.0), keepdims=True)
    denominator = jnp.sum(jnp.where(lane == 1, sums, 0.0), keepdims=True)
    return numerator / (denominator + EPSILON)


def sums_out(numerator, denominator, shape):
    lane = lax.broadcasted_iota(jnp.int32, shape, 1)
    return jnp.where(lane == 0, numerator, jnp.where(lane == 1, denominator, 0.0))


def weighted(field, weight, edge):
    blocks, columns = weight.shape
    return (field.reshape(blocks, edge, columns) * weight[:, None, :]).reshape(field.shape)


def pack_kernel(meta_ref, flags_ref, data_ref, out_ref, *, n_src, n_rcv):
    _, groups, _, edge, width = data_ref.shape
    pairs = width // (2 * edge)
    odd = mod(meta_ref[1], 2)
    placed = (odd, 1 - odd)
    for sigma in range(n_src):
        for u in range(groups):
            for pair in range(pairs):
                re = data_ref[0, u, sigma, :, pair * 2 * edge : (pair + 1) * 2 * edge]
                im = data_ref[1, u, sigma, :, pair * 2 * edge : (pair + 1) * 2 * edge]
                first = jnp.concatenate([re[:, :edge], im[:, :edge]], axis=1)
                second = jnp.concatenate([re[:, edge:], im[:, edge:]], axis=1)
                for side, block in ((0, first), (1, second)):
                    column = 2 * pair + side
                    source = sigma + n_src * u
                    seen = flags_ref[source, column] != 0
                    diff = (column - source) % n_rcv
                    q = diff // 2
                    turns = (source + diff) // n_rcv + (sigma + q) // n_src
                    near = (sigma + diff) % n_rcv < n_rcv // 2
                    slot = 2 * (diff % 2) + (u // 2 if near else u % 2)
                    dest = (sigma + q) % n_src * n_rcv + 2 * q + placed[(u + turns) % 2]
                    out_ref[dest, slot] = jnp.where(
                        seen, block, jnp.full_like(block, ABSENT)
                    )


def first_kernel(meta_ref, blocks_ref, left_ref, right_ref,
                 target_ref, w_ref, start_ref, grad_ref, product_ref, residual_ref,
                 *, n_src, n_rcv, slots, edge, per_src, per_rcv):
    src, pair, beta, band = meta_ref[0], meta_ref[2], meta_ref[3], meta_ref[4]
    total = n_src * per_src
    mids = left_ref.shape[0]
    groups = per_src // n_src
    half = n_rcv // 2
    tiles = target_ref.shape[0]
    width = 2 * edge
    per_tile = target_ref.shape[2] // width
    start_ref[...] = left_ref[:, pl.ds(beta, 1)].reshape(start_ref.shape)
    left_b = start_ref[...].astype(bf16)
    for tile in range(tiles):
        rows = slice(tile * per_tile * edge, (tile + 1) * per_tile * edge)
        stack = stacked(right_ref[rows, :], edge)
        product_ref[...] = nt(left_b, stack)
        for side in range(per_tile):
            column = tile * per_tile + side
            tau, t = column // slots, column % slots
            residue = 2 * pair + tau
            offset = n_rcv * t + residue - half * slots
            inside = jnp.abs(offset) <= band
            cols = slice(side * width, (side + 1) * width)
            for mm in range(mids):
                mid = src + n_src * (2 * mm + beta)
                source = mod(mid - (offset >> 1), total)
                receiver = mod(source + offset, total)
                u = div(mod(source, per_src), n_src)
                near = mod(mod(source, n_src) + residue, n_rcv) < half
                slot = 2 * tau + jnp.where(near, div(u, 2), mod(u, 2))
                message = div(source, per_src) * n_rcv + div(receiver, per_rcv)
                wide = blocks_ref[message, slot].astype(f32)
                keep = jnp.logical_and(wide < LIMIT, inside)
                at = slice(mm * edge, (mm + 1) * edge)
                target_ref[tile, at, cols] = jnp.where(keep, wide, 0.0).astype(bf16)
                w_ref[tile, mm : mm + 1, cols] = jnp.where(keep[0:1], 1.0, 0.0)
                residual_ref[at, cols] = jnp.where(
                    keep, product_ref[at, cols] - wide, 0.0
                ).astype(bf16)
        grad = nn(residual_ref[...], stack)
        grad_ref[...] = grad if tile == 0 else grad_ref[...] + grad


def spread_kernel(parts_ref, out_ref):
    total = jnp.sum(parts_ref[...], axis=0)
    out_ref[...] = jnp.broadcast_to(total[None], out_ref.shape)


def curve_kernel(left_ref, right_ref, w_ref, out_ref, *, edge, copies, by_left):
    left_b = left_ref[...].astype(bf16)
    mids = left_b.shape[0] // edge
    tiles, _, width = w_ref.shape
    total = jnp.zeros((mids, width), f32)
    for tile in range(tiles):
        curve = nt(left_b, stacked(tile_rows(right_ref, tile, w_ref), edge))
        squares = (curve * curve).reshape(mids, edge, width)
        total = total + jnp.sum(squares, axis=1) * w_ref[tile]
    grad = left_ref[...] if by_left else right_ref[...]
    numerator = jnp.sum(grad * grad, keepdims=True) * (1.0 / copies)
    out_ref[...] = sums_out(numerator, jnp.sum(total, keepdims=True), out_ref.shape)


def residual_of(target, weight, lefts, stacks, steps, edge):
    residual = nt(lefts[0], stacks[0]) - target.astype(f32)
    for left, stack, step in zip(lefts[1:], stacks[1:], steps):
        residual = residual - step * nt(left, stack)
    return weighted(residual, weight, edge).astype(bf16)


def tile_rows(ref, tile, w_ref):
    rows = w_ref.shape[2] // 2
    return ref[tile * rows : (tile + 1) * rows, :]


def left_update_kernel(meta_ref, sums_ref, target_ref, w_ref, start_ref, first_grad_ref,
                       right_ref, left_out_ref, out_ref, *, edge):
    step = step_of(sums_ref[...])
    start = start_ref[...]
    grad = first_grad_ref[...]
    new = start - step * grad
    left_out_ref[...] = new
    lefts = [start.astype(bf16), grad.astype(bf16)]
    new_b = new.astype(bf16)
    rows = w_ref.shape[2] // 2
    for tile in range(w_ref.shape[0]):
        stack = stacked(tile_rows(right_ref, tile, w_ref), edge)
        residual = residual_of(
            target_ref[tile], w_ref[tile], lefts, [stack, stack], [step], edge
        )
        out_ref[tile * rows : (tile + 1) * rows, :] = combined(tn(new_b, residual).T, edge)


def left_again_kernel(meta_ref, sums_ref, sums_r_ref, sums_now_ref, target_ref, w_ref, start_ref,
                      first_grad_ref, right_ref, left_ref, grad_ref, grad_r_ref, right_now_ref,
                      *refs, edge):
    *other_refs, given_ref, left_b_ref, left_out_ref, out_ref, own_ref, other_ref, sem_ref = refs
    beta = meta_ref[3]
    fetch = pltpu.make_async_copy(given_ref.at[:, 1 - beta], other_ref, sem_ref.at[0])
    own_out = pltpu.make_async_copy(own_ref, left_out_ref.at[:, beta], sem_ref.at[1])
    other_out = pltpu.make_async_copy(other_ref, left_out_ref.at[:, 1 - beta], sem_ref.at[2])
    fetch.start()
    steps = [step_of(ref[...]) for ref in (sums_ref, sums_r_ref, sums_now_ref)]
    new = left_ref[...] - steps[2] * grad_ref[...]
    own_ref[...] = new.reshape(own_ref.shape)
    own_out.start()
    fetch.wait()
    half = len(other_refs) // 2
    mids = other_ref.shape[0] // half
    for part in range(half):
        at = slice(part * mids, (part + 1) * mids)
        first, second = other_refs[part][...], other_refs[half + part][...]
        taken = other_ref[at].reshape(first.shape) - steps[0] * first - steps[2] * second
        other_ref[at] = taken.reshape((mids,) + other_ref.shape[1:])
    other_out.start()
    new_b = new.astype(bf16)
    left_b_ref[...] = new_b
    lefts = [ref[...].astype(bf16) for ref in (start_ref, first_grad_ref, left_ref, grad_ref)]
    rows = w_ref.shape[2] // 2
    for tile in range(w_ref.shape[0]):
        stack, stack_r, stack_now = [
            stacked(tile_rows(ref, tile, w_ref), edge)
            for ref in (right_ref, grad_r_ref, right_now_ref)
        ]
        residual = residual_of(
            target_ref[tile], w_ref[tile], lefts, [stack, stack, stack_r, stack_now], steps, edge
        )
        out_ref[tile * rows : (tile + 1) * rows, :] = combined(tn(new_b, residual).T, edge)
    own_out.wait()
    other_out.wait()


def right_update_kernel(meta_ref, sums_ref, sums_r_ref, target_ref, w_ref, start_ref,
                        first_grad_ref, right_ref, left_ref, grad_r_ref,
                        right_out_ref, grad_ref, *, edge):
    step = step_of(sums_ref[...])
    step_r = step_of(sums_r_ref[...])
    right_out_ref[...] = right_ref[...] - step_r * grad_r_ref[...]
    start = start_ref[...]
    lefts = [value.astype(bf16) for value in (start, first_grad_ref[...], left_ref[...])]
    for tile in range(w_ref.shape[0]):
        stack, stack_r, stack_now = [
            stacked(tile_rows(ref, tile, w_ref), edge)
            for ref in (right_ref, grad_r_ref, right_out_ref)
        ]
        residual = residual_of(
            target_ref[tile], w_ref[tile], lefts, [stack, stack, stack_r], [step, step_r], edge
        )
        grad = nn(residual, stack_now)
        grad_ref[...] = grad if tile == 0 else grad_ref[...] + grad


def right_last_kernel(meta_ref, sums_ref, grad_r_ref, right_ref, right_out_ref):
    own = right_out_ref.shape[0]
    rows = pl.ds(pl.multiple_of(meta_ref[3] * own, own), own)
    right_out_ref[...] = right_ref[rows, :] - step_of(sums_ref[...]) * grad_r_ref[rows, :]


def per_device(data, observed, band_width, left_factor, right_factor):
    n_src = lax.axis_size("src")
    n_pair = lax.axis_size("pair")
    n_rcv = 2 * n_pair
    devices = n_src * n_rcv
    per_src, per_rcv = observed.shape
    edge = data.shape[1] // per_src
    groups = per_src // n_src
    slots = right_factor.shape[0]
    rank2 = left_factor.shape[3]
    mids = per_src // 2
    rows = mids * edge
    own_cols = slots * edge
    cols = 2 * own_cols
    width = 4 * edge
    tiles = 2 * cols // width
    everyone = ("src", "pair", "beta")
    swap = [(0, 1), (1, 0)]

    src = lax.axis_index("src")
    pair = lax.axis_index("pair")
    beta = lax.axis_index("beta")
    meta = jnp.stack([src, 2 * pair + beta, pair, beta, band_width[0]]).astype(jnp.int32)

    own_right = right_factor.reshape(own_cols, rank2)
    other_right = lax.ppermute(own_right, "beta", swap)
    packed = pl.pallas_call(
        lambda *refs: pack_kernel(*refs, n_src=n_src, n_rcv=n_rcv),
        out_shape=jax.ShapeDtypeStruct((devices, groups, edge, 2 * edge), bf16),
        in_specs=[pl.BlockSpec(memory_space=pltpu.SMEM)] * 2
        + [pl.BlockSpec(memory_space=pltpu.VMEM)],
        out_specs=pl.BlockSpec(memory_space=pltpu.VMEM),
        compiler_params=params(),
        name="pack",
    )(meta, observed, data.reshape(2, groups, n_src, edge, data.shape[2]))
    right = jnp.concatenate([
        jnp.where(beta == 0, own_right, other_right),
        jnp.where(beta == 0, other_right, own_right),
    ])
    packed, right = lax.optimization_barrier((packed, right))
    arrived = lax.all_to_all(packed, everyone, split_axis=0, concat_axis=0, tiled=True)

    left_shape = jax.ShapeDtypeStruct((rows, rank2), f32)
    right_shape = jax.ShapeDtypeStruct((cols, rank2), f32)
    sums_shape = jax.ShapeDtypeStruct((devices, 128), f32)

    def call(kernel, name, out_shape, inputs, **kw):
        return pl.pallas_call(
            kernel,
            out_shape=out_shape,
            in_specs=[pl.BlockSpec(memory_space=pltpu.SMEM)]
            + [pl.BlockSpec(memory_space=pltpu.VMEM)] * inputs,
            compiler_params=params(),
            name=name,
            **kw,
        )

    target, weight, start, parts = call(
        lambda *refs: first_kernel(
            *refs, n_src=n_src, n_rcv=n_rcv, slots=slots, edge=edge,
            per_src=per_src, per_rcv=per_rcv,
        ),
        "first_gradient",
        (
            jax.ShapeDtypeStruct((tiles, rows, width), bf16),
            jax.ShapeDtypeStruct((tiles, mids, width), f32),
            left_shape,
            left_shape,
        ),
        3,
        scratch_shapes=[pltpu.VMEM((rows, width), f32), pltpu.VMEM((rows, width), bf16)],
    )(meta, arrived, left_factor.reshape(mids, 2, edge, rank2), right)

    def spread(parts, axis, count):
        split = parts.reshape(count, parts.shape[0] // count, rank2)
        landed = lax.all_to_all(split, axis, split_axis=0, concat_axis=0, tiled=True)
        copies = pl.pallas_call(
            spread_kernel,
            out_shape=jax.ShapeDtypeStruct(split.shape, f32),
            compiler_params=params(),
            name="sum_parts",
        )(landed)
        full = lax.all_to_all(copies, axis, split_axis=0, concat_axis=0, tiled=True)
        return full.reshape(parts.shape)

    def shared(left, right, by_left, copies):
        sums = pl.pallas_call(
            lambda *refs: curve_kernel(*refs, edge=edge, copies=copies, by_left=by_left),
            out_shape=sums_shape,
            compiler_params=params(),
            name="left_curve" if by_left else "right_curve",
        )(left, right, weight)
        return lax.all_to_all(sums, everyone, split_axis=0, concat_axis=0, tiled=True)

    def from_others(grad):
        return [
            lax.ppermute(
                grad[part * rows // 2 : (part + 1) * rows // 2], ("pair", "beta"),
                [(at, at - at % RING + (at + shift) % RING) for at in range(n_rcv)],
            )
            for part, shift in enumerate((1, -1))
        ]

    right_group = ("src", "beta")
    grad = spread(parts, "pair", n_pair)
    sums = shared(grad, right, True, n_pair)
    sums, others = lax.optimization_barrier((sums, from_others(grad)))
    left_one, parts_r = call(
        lambda *refs: left_update_kernel(*refs, edge=edge),
        "left_update", (left_shape, right_shape), 6,
    )(meta, sums, target, weight, start, grad, right)
    grad_r = spread(parts_r, right_group, 2 * n_src)
    sums_r = shared(left_one, grad_r, False, 2 * n_src)
    right_one, parts = call(
        lambda *refs: right_update_kernel(*refs, edge=edge),
        "right_update", (right_shape, left_shape), 9,
    )(meta, sums, sums_r, target, weight, start, grad, right, left_one, grad_r)
    grad_two = spread(parts, "pair", n_pair)
    sums_two = shared(grad_two, right_one, True, n_pair)
    sums_two, others_two = lax.optimization_barrier((sums_two, from_others(grad_two)))
    in_vmem = pl.BlockSpec(memory_space=pltpu.VMEM)
    left_two, left_out, parts_r = pl.pallas_call(
        lambda *refs: left_again_kernel(*refs, edge=edge),
        out_shape=(
            jax.ShapeDtypeStruct((rows, rank2), bf16),
            jax.ShapeDtypeStruct((mids, 2, edge, rank2), f32),
            right_shape,
        ),
        in_specs=[pl.BlockSpec(memory_space=pltpu.SMEM)] + [in_vmem] * 16
        + [pl.BlockSpec(memory_space=pltpu.HBM)],
        out_specs=(in_vmem, pl.BlockSpec(memory_space=pltpu.HBM), in_vmem),
        scratch_shapes=[pltpu.VMEM((mids, edge, rank2), f32)] * 2
        + [pltpu.SemaphoreType.DMA((3,))],
        compiler_params=params(),
        name="left_again",
    )(
        meta, sums, sums_r, sums_two, target, weight, start, grad, right, left_one,
        grad_two, grad_r, right_one, *others, *others_two,
        left_factor.reshape(mids, 2, edge, rank2),
    )
    grad_r_two = spread(parts_r, right_group, 2 * n_src)
    sums_r_two = shared(left_two, grad_r_two, False, 2 * n_src)
    right_out = call(
        right_last_kernel, "right_last", jax.ShapeDtypeStruct((own_cols, rank2), f32), 3,
    )(meta, sums_r_two, grad_r_two, right_one)
    return left_out.reshape(left_factor.shape), right_out.reshape(right_factor.shape)


def solution(mesh):
    n_src, n_rcv = mesh.shape["src"], mesh.shape["rcv"]
    split = jax.sharding.Mesh(
        mesh.devices.reshape(n_src, n_rcv // 2, 2), ("src", "pair", "beta")
    )
    rcv = ("pair", "beta")
    return jax.shard_map(
        per_device,
        mesh=split,
        in_specs=(
            P(None, "src", rcv),
            P("src", rcv),
            P(),
            P(None, "src", None, None),
            P(None, rcv, None, None),
        ),
        out_specs=(P(None, "src", None, None), P(None, rcv, None, None)),
        check_vma=False,
    )
```

```python
import jax
import jax.numpy as jnp
from jax import lax
from jax.experimental import pallas as pl
from jax.experimental.pallas import tpu as pltpu
from jax.sharding import PartitionSpec as P

EPSILON = 1e-06
REACH = 8
TAIL = 8
ABSENT = 1024.0
LIMIT = 512.0
VMEM = 24 * 1024 * 1024
f32 = jnp.float32
bf16 = jnp.bfloat16


def params():
    return pltpu.CompilerParams(vmem_limit_bytes=VMEM)


def mod(x, n):
    assert n & (n - 1) == 0
    return x & (n - 1)


def div(x, n):
    assert n & (n - 1) == 0
    return x >> (n.bit_length() - 1)


def nt(a, b):
    return lax.dot_general(a, b, (((1,), (1,)), ((), ())), preferred_element_type=f32)


def nn(a, b):
    return lax.dot_general(a, b, (((1,), (0,)), ((), ())), preferred_element_type=f32)


def tn(a, b):
    return lax.dot_general(a, b, (((0,), (0,)), ((), ())), preferred_element_type=f32)


def stacked(factor, edge):
    half = factor.shape[1] // 2
    rounded = factor.astype(bf16)
    turned = jnp.concatenate([-rounded[:, half:], rounded[:, :half]], axis=1)
    pieces = []
    for t in range(factor.shape[0] // edge):
        rows = slice(t * edge, (t + 1) * edge)
        pieces += [rounded[rows], turned[rows]]
    return jnp.concatenate(pieces, axis=0)


def combined(products, edge):
    half = products.shape[1] // 2
    pieces = []
    for t in range(products.shape[0] // (2 * edge)):
        upper = products[2 * t * edge : (2 * t + 1) * edge]
        lower = products[(2 * t + 1) * edge : (2 * t + 2) * edge]
        pieces.append(jnp.concatenate(
            [upper[:, :half] + lower[:, half:], upper[:, half:] - lower[:, :half]], axis=1
        ))
    return jnp.concatenate(pieces, axis=0)


def step_of(sums):
    lane = lax.broadcasted_iota(jnp.int32, sums.shape, 1)
    numerator = jnp.sum(jnp.where(lane == 0, sums, 0.0), keepdims=True)
    denominator = jnp.sum(jnp.where(lane == 1, sums, 0.0), keepdims=True)
    return numerator / (denominator + EPSILON)


def sums_out(numerator, denominator, shape):
    lane = lax.broadcasted_iota(jnp.int32, shape, 1)
    return jnp.where(lane == 0, numerator, jnp.where(lane == 1, denominator, 0.0))


def weighted(field, weight, edge):
    blocks, columns = weight.shape
    return (field.reshape(blocks, edge, columns) * weight[:, None, :]).reshape(field.shape)


def power(level):
    found = jnp.full_like(level, 2.0 ** (-8 * REACH))
    for k in range(1 - REACH, REACH + 1):
        found = jnp.where(level >= k, 2.0 ** (8 * k), found)
    return found


def encode(values, out_ref):
    count, padded, width = out_ref.shape
    rows = padded - TAIL
    peak = jnp.max(jnp.abs(values), keepdims=True)
    level = jnp.full_like(peak, -REACH)
    for k in range(1 - REACH, REACH + 1):
        level = jnp.where(peak >= 2.0 ** (8 * k + 7), float(k), level)
    scaled = (values * power(-level)).reshape(-1, rows, width)
    out_ref[:, :rows] = jnp.broadcast_to(scaled, (count, rows, width))
    out_ref[:, rows:] = jnp.broadcast_to(level[None], (count, TAIL, width))


def decode(message_ref):
    rows = message_ref.shape[1] - TAIL
    return message_ref[:, :rows] * power(message_ref[:, rows : rows + 1])


def pack_kernel(meta_ref, flags_ref, data_ref, out_ref, *, n_src, n_rcv):
    _, groups, _, edge, width = data_ref.shape
    pairs = width // (2 * edge)
    odd = mod(meta_ref[1], 2)
    placed = (odd, 1 - odd)
    for sigma in range(n_src):
        for u in range(groups):
            for pair in range(pairs):
                re = data_ref[0, u, sigma, :, pair * 2 * edge : (pair + 1) * 2 * edge]
                im = data_ref[1, u, sigma, :, pair * 2 * edge : (pair + 1) * 2 * edge]
                first = jnp.concatenate([re[:, :edge], im[:, :edge]], axis=1)
                second = jnp.concatenate([re[:, edge:], im[:, edge:]], axis=1)
                for side, block in ((0, first), (1, second)):
                    column = 2 * pair + side
                    source = sigma + n_src * u
                    seen = flags_ref[source, column] != 0
                    diff = (column - source) % n_rcv
                    q = diff // 2
                    turns = (source + diff) // n_rcv + (sigma + q) // n_src
                    near = (sigma + diff) % n_rcv < n_rcv // 2
                    slot = 2 * (diff % 2) + (u // 2 if near else u % 2)
                    dest = (sigma + q) % n_src * n_rcv + 2 * q + placed[(u + turns) % 2]
                    out_ref[dest, slot] = jnp.where(
                        seen, block, jnp.full_like(block, ABSENT)
                    )


def first_kernel(meta_ref, blocks_ref, left_ref, right_ref,
                 target_ref, w_ref, start_ref, out_ref, product_ref, residual_ref, grad_ref,
                 *, n_src, n_rcv, slots, edge, per_src, per_rcv):
    src, pair, beta, band = meta_ref[0], meta_ref[2], meta_ref[3], meta_ref[4]
    total = n_src * per_src
    mids = left_ref.shape[0]
    groups = per_src // n_src
    half = n_rcv // 2
    tiles = target_ref.shape[0]
    width = 2 * edge
    per_tile = target_ref.shape[2] // width
    start_ref[...] = left_ref[:, pl.ds(beta, 1)].reshape(start_ref.shape)
    left_b = start_ref[...].astype(bf16)
    for tile in range(tiles):
        rows = slice(tile * per_tile * edge, (tile + 1) * per_tile * edge)
        stack = stacked(right_ref[rows, :], edge)
        product_ref[...] = nt(left_b, stack)
        for side in range(per_tile):
            column = tile * per_tile + side
            tau, t = column // slots, column % slots
            residue = 2 * pair + tau
            offset = n_rcv * t + residue - half * slots
            inside = jnp.abs(offset) <= band
            cols = slice(side * width, (side + 1) * width)
            for mm in range(mids):
                mid = src + n_src * (2 * mm + beta)
                source = mod(mid - (offset >> 1), total)
                receiver = mod(source + offset, total)
                u = div(mod(source, per_src), n_src)
                near = mod(mod(source, n_src) + residue, n_rcv) < half
                slot = 2 * tau + jnp.where(near, div(u, 2), mod(u, 2))
                message = div(source, per_src) * n_rcv + div(receiver, per_rcv)
                wide = blocks_ref[message, slot].astype(f32)
                keep = jnp.logical_and(wide < LIMIT, inside)
                at = slice(mm * edge, (mm + 1) * edge)
                target_ref[tile, at, cols] = jnp.where(keep, wide, 0.0).astype(bf16)
                w_ref[tile, mm : mm + 1, cols] = jnp.where(keep[0:1], 1.0, 0.0)
                residual_ref[at, cols] = jnp.where(
                    keep, product_ref[at, cols] - wide, 0.0
                ).astype(bf16)
        grad = nn(residual_ref[...], stack)
        grad_ref[...] = grad if tile == 0 else grad_ref[...] + grad
    encode(grad_ref[...], out_ref)


def sum_kernel(parts_ref, out_ref):
    encode(jnp.sum(decode(parts_ref), axis=0), out_ref)


def curve_kernel(message_ref, factor_ref, w_ref, out_ref, grad_ref, *, edge, copies, by_left):
    grad_ref[...] = decode(message_ref).reshape(grad_ref.shape)
    left_ref, right_ref = (grad_ref, factor_ref) if by_left else (factor_ref, grad_ref)
    left_b = left_ref[...].astype(bf16)
    mids = left_b.shape[0] // edge
    tiles, _, width = w_ref.shape
    total = jnp.zeros((mids, width), f32)
    for tile in range(tiles):
        curve = nt(left_b, stacked(tile_rows(right_ref, tile, w_ref), edge))
        squares = (curve * curve).reshape(mids, edge, width)
        total = total + jnp.sum(squares, axis=1) * w_ref[tile]
    grad = grad_ref[...]
    numerator = jnp.sum(grad * grad, keepdims=True) * (1.0 / copies)
    out_ref[...] = sums_out(numerator, jnp.sum(total, keepdims=True), out_ref.shape)


def residual_of(target, weight, lefts, stacks, steps, edge):
    residual = nt(lefts[0], stacks[0]) - target.astype(f32)
    for left, stack, step in zip(lefts[1:], stacks[1:], steps):
        residual = residual - step * nt(left, stack)
    return weighted(residual, weight, edge).astype(bf16)


def tile_rows(ref, tile, w_ref):
    rows = w_ref.shape[2] // 2
    return ref[tile * rows : (tile + 1) * rows, :]


def left_update_kernel(meta_ref, sums_ref, target_ref, w_ref, start_ref, first_grad_ref,
                       right_ref, left_out_ref, out_ref, parts_ref, *, edge):
    step = step_of(sums_ref[...])
    start = start_ref[...]
    grad = first_grad_ref[...]
    new = start - step * grad
    left_out_ref[...] = new
    lefts = [start.astype(bf16), grad.astype(bf16)]
    new_b = new.astype(bf16)
    rows = w_ref.shape[2] // 2
    for tile in range(w_ref.shape[0]):
        stack = stacked(tile_rows(right_ref, tile, w_ref), edge)
        residual = residual_of(
            target_ref[tile], w_ref[tile], lefts, [stack, stack], [step], edge
        )
        parts_ref[tile * rows : (tile + 1) * rows, :] = combined(tn(new_b, residual).T, edge)
    encode(parts_ref[...], out_ref)


def left_again_kernel(meta_ref, sums_ref, sums_r_ref, sums_now_ref, target_ref, w_ref, start_ref,
                      first_grad_ref, right_ref, left_ref, grad_ref, grad_r_ref, right_now_ref,
                      *refs, edge):
    (first_ref, second_ref, given_ref, left_b_ref, left_out_ref, out_ref,
     own_ref, other_ref, parts_ref, sem_ref) = refs
    beta = meta_ref[3]
    fetch = pltpu.make_async_copy(given_ref.at[:, 1 - beta], other_ref, sem_ref.at[0])
    own_out = pltpu.make_async_copy(own_ref, left_out_ref.at[:, beta], sem_ref.at[1])
    other_out = pltpu.make_async_copy(other_ref, left_out_ref.at[:, 1 - beta], sem_ref.at[2])
    fetch.start()
    steps = [step_of(ref[...]) for ref in (sums_ref, sums_r_ref, sums_now_ref)]
    new = left_ref[...] - steps[2] * grad_ref[...]
    own_ref[...] = new.reshape(own_ref.shape)
    own_out.start()
    fetch.wait()
    taken = other_ref[...].reshape(left_ref.shape)
    for step, ref in ((steps[0], first_ref), (steps[2], second_ref)):
        taken = taken - step * decode(ref).reshape(taken.shape)
    other_ref[...] = taken.reshape(other_ref.shape)
    other_out.start()
    new_b = new.astype(bf16)
    left_b_ref[...] = new_b
    lefts = [ref[...].astype(bf16) for ref in (start_ref, first_grad_ref, left_ref, grad_ref)]
    rows = w_ref.shape[2] // 2
    for tile in range(w_ref.shape[0]):
        stack, stack_r, stack_now = [
            stacked(tile_rows(ref, tile, w_ref), edge)
            for ref in (right_ref, grad_r_ref, right_now_ref)
        ]
        residual = residual_of(
            target_ref[tile], w_ref[tile], lefts, [stack, stack, stack_r, stack_now], steps, edge
        )
        parts_ref[tile * rows : (tile + 1) * rows, :] = combined(tn(new_b, residual).T, edge)
    encode(parts_ref[...], out_ref)
    own_out.wait()
    other_out.wait()


def right_update_kernel(meta_ref, sums_ref, sums_r_ref, target_ref, w_ref, start_ref,
                        first_grad_ref, right_ref, left_ref, grad_r_ref,
                        right_out_ref, out_ref, grad_ref, *, edge):
    step = step_of(sums_ref[...])
    step_r = step_of(sums_r_ref[...])
    right_out_ref[...] = right_ref[...] - step_r * grad_r_ref[...]
    start = start_ref[...]
    lefts = [value.astype(bf16) for value in (start, first_grad_ref[...], left_ref[...])]
    for tile in range(w_ref.shape[0]):
        stack, stack_r, stack_now = [
            stacked(tile_rows(ref, tile, w_ref), edge)
            for ref in (right_ref, grad_r_ref, right_out_ref)
        ]
        residual = residual_of(
            target_ref[tile], w_ref[tile], lefts, [stack, stack, stack_r], [step, step_r], edge
        )
        grad = nn(residual, stack_now)
        grad_ref[...] = grad if tile == 0 else grad_ref[...] + grad
    encode(grad_ref[...], out_ref)


def right_last_kernel(meta_ref, sums_ref, grad_r_ref, right_ref, right_out_ref):
    own = right_out_ref.shape[0]
    rows = pl.ds(pl.multiple_of(meta_ref[3] * own, own), own)
    right_out_ref[...] = right_ref[rows, :] - step_of(sums_ref[...]) * grad_r_ref[rows, :]


def per_device(data, observed, band_width, left_factor, right_factor):
    n_src = lax.axis_size("src")
    n_pair = lax.axis_size("pair")
    n_rcv = 2 * n_pair
    devices = n_src * n_rcv
    per_src, per_rcv = observed.shape
    edge = data.shape[1] // per_src
    groups = per_src // n_src
    slots = right_factor.shape[0]
    rank2 = left_factor.shape[3]
    mids = per_src // 2
    rows = mids * edge
    own_cols = slots * edge
    cols = 2 * own_cols
    width = 4 * edge
    tiles = 2 * cols // width
    everyone = ("src", "pair", "beta")
    swap = [(0, 1), (1, 0)]

    src = lax.axis_index("src")
    pair = lax.axis_index("pair")
    beta = lax.axis_index("beta")
    meta = jnp.stack([src, 2 * pair + beta, pair, beta, band_width[0]]).astype(jnp.int32)

    own_right = right_factor.reshape(own_cols, rank2)
    other_right = lax.ppermute(own_right, "beta", swap)
    packed = pl.pallas_call(
        lambda *refs: pack_kernel(*refs, n_src=n_src, n_rcv=n_rcv),
        out_shape=jax.ShapeDtypeStruct((devices, groups, edge, 2 * edge), bf16),
        in_specs=[pl.BlockSpec(memory_space=pltpu.SMEM)] * 2
        + [pl.BlockSpec(memory_space=pltpu.VMEM)],
        out_specs=pl.BlockSpec(memory_space=pltpu.VMEM),
        compiler_params=params(),
        name="pack",
    )(meta, observed, data.reshape(2, groups, n_src, edge, data.shape[2]))
    right = jnp.concatenate([
        jnp.where(beta == 0, own_right, other_right),
        jnp.where(beta == 0, other_right, own_right),
    ])
    packed, right = lax.optimization_barrier((packed, right))
    arrived = lax.all_to_all(packed, everyone, split_axis=0, concat_axis=0, tiled=True)

    left_shape = jax.ShapeDtypeStruct((rows, rank2), f32)
    right_shape = jax.ShapeDtypeStruct((cols, rank2), f32)

    def parts_shape(count, length):
        return jax.ShapeDtypeStruct((count, length // count + TAIL, rank2), f32)

    left_parts = parts_shape(n_pair, rows)
    right_parts = parts_shape(2 * n_src, cols)
    sums_shape = jax.ShapeDtypeStruct((devices, 128), f32)

    def call(kernel, name, out_shape, inputs, **kw):
        return pl.pallas_call(
            kernel,
            out_shape=out_shape,
            in_specs=[pl.BlockSpec(memory_space=pltpu.SMEM)]
            + [pl.BlockSpec(memory_space=pltpu.VMEM)] * inputs,
            compiler_params=params(),
            name=name,
            **kw,
        )

    target, weight, start, parts = call(
        lambda *refs: first_kernel(
            *refs, n_src=n_src, n_rcv=n_rcv, slots=slots, edge=edge,
            per_src=per_src, per_rcv=per_rcv,
        ),
        "first_gradient",
        (
            jax.ShapeDtypeStruct((tiles, rows, width), bf16),
            jax.ShapeDtypeStruct((tiles, mids, width), f32),
            left_shape,
            left_parts,
        ),
        3,
        scratch_shapes=[
            pltpu.VMEM((rows, width), f32), pltpu.VMEM((rows, width), bf16),
            pltpu.VMEM((rows, rank2), f32),
        ],
    )(meta, arrived, left_factor.reshape(mids, 2, edge, rank2), right)

    def send(parts, axis):
        return lax.all_to_all(
            parts.astype(jnp.float16), axis, split_axis=0, concat_axis=0, tiled=True
        )

    def spread(parts, axis):
        summed = pl.pallas_call(
            sum_kernel,
            out_shape=jax.ShapeDtypeStruct(parts.shape, f32),
            compiler_params=params(),
            name="sum_parts",
        )(send(parts, axis).astype(f32))
        return send(summed, axis)

    def shared(message, factor, by_left, copies):
        sums, grad = pl.pallas_call(
            lambda *refs: curve_kernel(*refs, edge=edge, copies=copies, by_left=by_left),
            out_shape=(sums_shape, left_shape if by_left else right_shape),
            compiler_params=params(),
            name="left_curve" if by_left else "right_curve",
        )(message.astype(f32), factor, weight)
        sums = lax.all_to_all(sums, everyone, split_axis=0, concat_axis=0, tiled=True)
        return sums, grad

    def shared_left(parts, factor, *before):
        message = spread(parts, "pair")
        other = lax.ppermute(message, "beta", swap)
        sums, grad = shared(message, factor, True, n_pair)
        sums, *others = lax.optimization_barrier((sums, *before, other))
        return sums, grad, *others

    right_group = ("src", "beta")
    sums, grad, other = shared_left(parts, right)
    left_one, parts_r = call(
        lambda *refs: left_update_kernel(*refs, edge=edge),
        "left_update", (left_shape, right_parts), 6,
        scratch_shapes=[pltpu.VMEM((cols, rank2), f32)],
    )(meta, sums, target, weight, start, grad, right)
    sums_r, grad_r = shared(spread(parts_r, right_group), left_one, False, 2 * n_src)
    right_one, parts = call(
        lambda *refs: right_update_kernel(*refs, edge=edge),
        "right_update", (right_shape, left_parts), 9,
        scratch_shapes=[pltpu.VMEM((rows, rank2), f32)],
    )(meta, sums, sums_r, target, weight, start, grad, right, left_one, grad_r)
    sums_two, grad_two, other, other_two = shared_left(parts, right_one, other)
    in_vmem = pl.BlockSpec(memory_space=pltpu.VMEM)
    left_two, left_out, parts_r = pl.pallas_call(
        lambda *refs: left_again_kernel(*refs, edge=edge),
        out_shape=(
            jax.ShapeDtypeStruct((rows, rank2), bf16),
            jax.ShapeDtypeStruct((mids, 2, edge, rank2), f32),
            right_parts,
        ),
        in_specs=[pl.BlockSpec(memory_space=pltpu.SMEM)] + [in_vmem] * 14
        + [pl.BlockSpec(memory_space=pltpu.HBM)],
        out_specs=(in_vmem, pl.BlockSpec(memory_space=pltpu.HBM), in_vmem),
        scratch_shapes=[pltpu.VMEM((mids, edge, rank2), f32)] * 2
        + [pltpu.VMEM((cols, rank2), f32), pltpu.SemaphoreType.DMA((3,))],
        compiler_params=params(),
        name="left_again",
    )(
        meta, sums, sums_r, sums_two, target, weight, start, grad, right, left_one,
        grad_two, grad_r, right_one, other.astype(f32), other_two.astype(f32),
        left_factor.reshape(mids, 2, edge, rank2),
    )
    sums_r_two, grad_r_two = shared(spread(parts_r, right_group), left_two, False, 2 * n_src)
    right_out = call(
        right_last_kernel, "right_last", jax.ShapeDtypeStruct((own_cols, rank2), f32), 3,
    )(meta, sums_r_two, grad_r_two, right_one)
    return left_out.reshape(left_factor.shape), right_out.reshape(right_factor.shape)


def solution(mesh):
    n_src, n_rcv = mesh.shape["src"], mesh.shape["rcv"]
    split = jax.sharding.Mesh(
        mesh.devices.reshape(n_src, n_rcv // 2, 2), ("src", "pair", "beta")
    )
    rcv = ("pair", "beta")
    return jax.shard_map(
        per_device,
        mesh=split,
        in_specs=(
            P(None, "src", rcv),
            P("src", rcv),
            P(),
            P(None, "src", None, None),
            P(None, rcv, None, None),
        ),
        out_specs=(P(None, "src", None, None), P(None, rcv, None, None)),
        check_vma=False,
    )
```

```python
import jax
import jax.numpy as jnp
from jax import lax
from jax.experimental import pallas as pl
from jax.experimental.pallas import tpu as pltpu
from jax.sharding import PartitionSpec as P

EPSILON = 1e-06
REACH = 8
TAIL = 8
ABSENT = 1024.0
LIMIT = 512.0
VMEM = 24 * 1024 * 1024
f32 = jnp.float32
bf16 = jnp.bfloat16


def params():
    return pltpu.CompilerParams(vmem_limit_bytes=VMEM)


def mod(x, n):
    assert n & (n - 1) == 0
    return x & (n - 1)


def div(x, n):
    assert n & (n - 1) == 0
    return x >> (n.bit_length() - 1)


def nt(a, b):
    return lax.dot_general(a, b, (((1,), (1,)), ((), ())), preferred_element_type=f32)


def nn(a, b):
    return lax.dot_general(a, b, (((1,), (0,)), ((), ())), preferred_element_type=f32)


def tn(a, b):
    return lax.dot_general(a, b, (((0,), (0,)), ((), ())), preferred_element_type=f32)


def stacked(factor, edge):
    half = factor.shape[1] // 2
    rounded = factor.astype(bf16)
    turned = jnp.concatenate([-rounded[:, half:], rounded[:, :half]], axis=1)
    pieces = []
    for t in range(factor.shape[0] // edge):
        rows = slice(t * edge, (t + 1) * edge)
        pieces += [rounded[rows], turned[rows]]
    return jnp.concatenate(pieces, axis=0)


def combined(products, edge):
    half = products.shape[1] // 2
    pieces = []
    for t in range(products.shape[0] // (2 * edge)):
        upper = products[2 * t * edge : (2 * t + 1) * edge]
        lower = products[(2 * t + 1) * edge : (2 * t + 2) * edge]
        pieces.append(jnp.concatenate(
            [upper[:, :half] + lower[:, half:], upper[:, half:] - lower[:, :half]], axis=1
        ))
    return jnp.concatenate(pieces, axis=0)


def step_of(sums):
    lane = lax.broadcasted_iota(jnp.int32, sums.shape, 1)
    numerator = jnp.sum(jnp.where(lane == 0, sums, 0.0), keepdims=True)
    denominator = jnp.sum(jnp.where(lane == 1, sums, 0.0), keepdims=True)
    return numerator / (denominator + EPSILON)


def sums_out(numerator, denominator, shape):
    lane = lax.broadcasted_iota(jnp.int32, shape, 1)
    return jnp.where(lane == 0, numerator, jnp.where(lane == 1, denominator, 0.0))


def weighted(field, weight, edge):
    blocks, columns = weight.shape
    return (field.reshape(blocks, edge, columns) * weight[:, None, :]).reshape(field.shape)


def power(level):
    found = jnp.full_like(level, 2.0 ** (-8 * REACH))
    for k in range(1 - REACH, REACH + 1):
        found = jnp.where(level >= k, 2.0 ** (8 * k), found)
    return found


def steady(values):
    near = values.astype(bf16).astype(f32)
    spread = values * (2.0 ** 13 + 1.0)
    rounded = spread - (spread - values)
    same = rounded.astype(bf16).astype(f32) == near
    return jnp.where(same, values, near + 0.8 * (values - near))


def encode(values, out_ref, last=False):
    count, padded, width = out_ref.shape
    rows = padded - TAIL
    peak = jnp.max(jnp.abs(values), keepdims=True)
    level = jnp.full_like(peak, -REACH)
    for k in range(1 - REACH, REACH + 1):
        level = jnp.where(peak >= 2.0 ** (8 * k + 7), float(k), level)
    scaled = values * power(-level)
    scaled = (steady(scaled) if last else scaled).reshape(-1, rows, width)
    out_ref[:, :rows] = jnp.broadcast_to(scaled, (count, rows, width))
    out_ref[:, rows:] = jnp.broadcast_to(level[None], (count, TAIL, width))


def decode(message_ref):
    rows = message_ref.shape[1] - TAIL
    return message_ref[:, :rows] * power(message_ref[:, rows : rows + 1])


def pack_kernel(meta_ref, flags_ref, data_ref, out_ref, *, n_src, n_rcv):
    _, groups, _, edge, width = data_ref.shape
    pairs = width // (2 * edge)
    odd = mod(meta_ref[1], 2)
    placed = (odd, 1 - odd)
    for sigma in range(n_src):
        for u in range(groups):
            for pair in range(pairs):
                re = data_ref[0, u, sigma, :, pair * 2 * edge : (pair + 1) * 2 * edge]
                im = data_ref[1, u, sigma, :, pair * 2 * edge : (pair + 1) * 2 * edge]
                first = jnp.concatenate([re[:, :edge], im[:, :edge]], axis=1)
                second = jnp.concatenate([re[:, edge:], im[:, edge:]], axis=1)
                for side, block in ((0, first), (1, second)):
                    column = 2 * pair + side
                    source = sigma + n_src * u
                    seen = flags_ref[source, column] != 0
                    diff = (column - source) % n_rcv
                    q = diff // 2
                    turns = (source + diff) // n_rcv + (sigma + q) // n_src
                    near = (sigma + diff) % n_rcv < n_rcv // 2
                    slot = 2 * (diff % 2) + (u // 2 if near else u % 2)
                    dest = (sigma + q) % n_src * n_rcv + 2 * q + placed[(u + turns) % 2]
                    out_ref[dest, slot] = jnp.where(
                        seen, block, jnp.full_like(block, ABSENT)
                    )


def first_kernel(meta_ref, blocks_ref, left_ref, right_ref,
                 target_ref, w_ref, start_ref, out_ref, product_ref, residual_ref, grad_ref,
                 *, n_src, n_rcv, slots, edge, per_src, per_rcv):
    src, pair, beta, band = meta_ref[0], meta_ref[2], meta_ref[3], meta_ref[4]
    total = n_src * per_src
    mids = left_ref.shape[0]
    groups = per_src // n_src
    half = n_rcv // 2
    tiles = target_ref.shape[0]
    width = 2 * edge
    per_tile = target_ref.shape[2] // width
    start_ref[...] = left_ref[:, pl.ds(beta, 1)].reshape(start_ref.shape)
    left_b = start_ref[...].astype(bf16)
    for tile in range(tiles):
        rows = slice(tile * per_tile * edge, (tile + 1) * per_tile * edge)
        stack = stacked(right_ref[rows, :], edge)
        product_ref[...] = nt(left_b, stack)
        for side in range(per_tile):
            column = tile * per_tile + side
            tau, t = column // slots, column % slots
            residue = 2 * pair + tau
            offset = n_rcv * t + residue - half * slots
            inside = jnp.abs(offset) <= band
            cols = slice(side * width, (side + 1) * width)
            for mm in range(mids):
                mid = src + n_src * (2 * mm + beta)
                source = mod(mid - (offset >> 1), total)
                receiver = mod(source + offset, total)
                u = div(mod(source, per_src), n_src)
                near = mod(mod(source, n_src) + residue, n_rcv) < half
                slot = 2 * tau + jnp.where(near, div(u, 2), mod(u, 2))
                message = div(source, per_src) * n_rcv + div(receiver, per_rcv)
                wide = blocks_ref[message, slot].astype(f32)
                keep = jnp.logical_and(wide < LIMIT, inside)
                at = slice(mm * edge, (mm + 1) * edge)
                target_ref[tile, at, cols] = jnp.where(keep, wide, 0.0).astype(bf16)
                w_ref[tile, mm : mm + 1, cols] = jnp.where(keep[0:1], 1.0, 0.0)
                residual_ref[at, cols] = jnp.where(
                    keep, product_ref[at, cols] - wide, 0.0
                ).astype(bf16)
        grad = nn(residual_ref[...], stack)
        grad_ref[...] = grad if tile == 0 else grad_ref[...] + grad
    encode(grad_ref[...], out_ref)


def sum_kernel(parts_ref, out_ref):
    encode(jnp.sum(decode(parts_ref), axis=0), out_ref, last=True)


def curve_kernel(message_ref, factor_ref, w_ref, out_ref, grad_ref, *, edge, copies, by_left):
    grad_ref[...] = decode(message_ref).reshape(grad_ref.shape)
    left_ref, right_ref = (grad_ref, factor_ref) if by_left else (factor_ref, grad_ref)
    left_b = left_ref[...].astype(bf16)
    mids = left_b.shape[0] // edge
    tiles, _, width = w_ref.shape
    total = jnp.zeros((mids, width), f32)
    for tile in range(tiles):
        curve = nt(left_b, stacked(tile_rows(right_ref, tile, w_ref), edge))
        squares = (curve * curve).reshape(mids, edge, width)
        total = total + jnp.sum(squares, axis=1) * w_ref[tile]
    grad = grad_ref[...]
    numerator = jnp.sum(grad * grad, keepdims=True) * (1.0 / copies)
    out_ref[...] = sums_out(numerator, jnp.sum(total, keepdims=True), out_ref.shape)


def residual_of(target, weight, lefts, stacks, steps, edge):
    residual = nt(lefts[0], stacks[0]) - target.astype(f32)
    for left, stack, step in zip(lefts[1:], stacks[1:], steps):
        residual = residual - step * nt(left, stack)
    return weighted(residual, weight, edge).astype(bf16)


def tile_rows(ref, tile, w_ref):
    rows = w_ref.shape[2] // 2
    return ref[tile * rows : (tile + 1) * rows, :]


def left_update_kernel(meta_ref, sums_ref, target_ref, w_ref, start_ref, first_grad_ref,
                       right_ref, left_out_ref, out_ref, parts_ref, *, edge):
    step = step_of(sums_ref[...])
    start = start_ref[...]
    grad = first_grad_ref[...]
    new = start - step * grad
    left_out_ref[...] = new
    lefts = [start.astype(bf16), grad.astype(bf16)]
    new_b = new.astype(bf16)
    rows = w_ref.shape[2] // 2
    for tile in range(w_ref.shape[0]):
        stack = stacked(tile_rows(right_ref, tile, w_ref), edge)
        residual = residual_of(
            target_ref[tile], w_ref[tile], lefts, [stack, stack], [step], edge
        )
        parts_ref[tile * rows : (tile + 1) * rows, :] = combined(tn(new_b, residual).T, edge)
    encode(parts_ref[...], out_ref)


def left_again_kernel(meta_ref, sums_ref, sums_r_ref, sums_now_ref, target_ref, w_ref, start_ref,
                      first_grad_ref, right_ref, left_ref, grad_ref, grad_r_ref, right_now_ref,
                      *refs, edge):
    (first_ref, second_ref, given_ref, left_b_ref, left_out_ref, out_ref,
     own_ref, other_ref, parts_ref, sem_ref) = refs
    beta = meta_ref[3]
    fetch = pltpu.make_async_copy(given_ref.at[:, 1 - beta], other_ref, sem_ref.at[0])
    own_out = pltpu.make_async_copy(own_ref, left_out_ref.at[:, beta], sem_ref.at[1])
    other_out = pltpu.make_async_copy(other_ref, left_out_ref.at[:, 1 - beta], sem_ref.at[2])
    fetch.start()
    steps = [step_of(ref[...]) for ref in (sums_ref, sums_r_ref, sums_now_ref)]
    new = left_ref[...] - steps[2] * grad_ref[...]
    own_ref[...] = new.reshape(own_ref.shape)
    own_out.start()
    new_b = new.astype(bf16)
    left_b_ref[...] = new_b
    lefts = [ref[...].astype(bf16) for ref in (start_ref, first_grad_ref, left_ref, grad_ref)]
    rows = w_ref.shape[2] // 2
    for tile in range(w_ref.shape[0]):
        stack, stack_r, stack_now = [
            stacked(tile_rows(ref, tile, w_ref), edge)
            for ref in (right_ref, grad_r_ref, right_now_ref)
        ]
        if tile == 1:
            fetch.wait()
            taken = other_ref[...].reshape(left_ref.shape)
            for step, ref in ((steps[0], first_ref), (steps[2], second_ref)):
                taken = taken - step * decode(ref).reshape(taken.shape)
            other_ref[...] = taken.reshape(other_ref.shape)
            other_out.start()
        residual = residual_of(
            target_ref[tile], w_ref[tile], lefts, [stack, stack, stack_r, stack_now], steps, edge
        )
        parts_ref[tile * rows : (tile + 1) * rows, :] = combined(tn(new_b, residual).T, edge)
    encode(parts_ref[...], out_ref)
    own_out.wait()
    other_out.wait()


def right_update_kernel(meta_ref, sums_ref, sums_r_ref, target_ref, w_ref, start_ref,
                        first_grad_ref, right_ref, left_ref, grad_r_ref,
                        right_out_ref, out_ref, grad_ref, *, edge):
    step = step_of(sums_ref[...])
    step_r = step_of(sums_r_ref[...])
    right_out_ref[...] = right_ref[...] - step_r * grad_r_ref[...]
    start = start_ref[...]
    lefts = [value.astype(bf16) for value in (start, first_grad_ref[...], left_ref[...])]
    for tile in range(w_ref.shape[0]):
        stack, stack_r, stack_now = [
            stacked(tile_rows(ref, tile, w_ref), edge)
            for ref in (right_ref, grad_r_ref, right_out_ref)
        ]
        residual = residual_of(
            target_ref[tile], w_ref[tile], lefts, [stack, stack, stack_r], [step, step_r], edge
        )
        grad = nn(residual, stack_now)
        grad_ref[...] = grad if tile == 0 else grad_ref[...] + grad
    encode(grad_ref[...], out_ref)


def right_last_kernel(meta_ref, sums_ref, grad_r_ref, right_ref, right_out_ref):
    own = right_out_ref.shape[0]
    rows = pl.ds(pl.multiple_of(meta_ref[3] * own, own), own)
    right_out_ref[...] = right_ref[rows, :] - step_of(sums_ref[...]) * grad_r_ref[rows, :]


def per_device(data, observed, band_width, left_factor, right_factor):
    n_src = lax.axis_size("src")
    n_pair = lax.axis_size("pair")
    n_rcv = 2 * n_pair
    devices = n_src * n_rcv
    per_src, per_rcv = observed.shape
    edge = data.shape[1] // per_src
    groups = per_src // n_src
    slots = right_factor.shape[0]
    rank2 = left_factor.shape[3]
    mids = per_src // 2
    rows = mids * edge
    own_cols = slots * edge
    cols = 2 * own_cols
    width = 4 * edge
    tiles = 2 * cols // width
    everyone = ("src", "pair", "beta")
    swap = [(0, 1), (1, 0)]

    src = lax.axis_index("src")
    pair = lax.axis_index("pair")
    beta = lax.axis_index("beta")
    meta = jnp.stack([src, 2 * pair + beta, pair, beta, band_width[0]]).astype(jnp.int32)

    own_right = right_factor.reshape(own_cols, rank2)
    other_right = lax.ppermute(own_right, "beta", swap)
    packed = pl.pallas_call(
        lambda *refs: pack_kernel(*refs, n_src=n_src, n_rcv=n_rcv),
        out_shape=jax.ShapeDtypeStruct((devices, groups, edge, 2 * edge), bf16),
        in_specs=[pl.BlockSpec(memory_space=pltpu.SMEM)] * 2
        + [pl.BlockSpec(memory_space=pltpu.VMEM)],
        out_specs=pl.BlockSpec(memory_space=pltpu.VMEM),
        compiler_params=params(),
        name="pack",
    )(meta, observed, data.reshape(2, groups, n_src, edge, data.shape[2]))
    right = jnp.concatenate([
        jnp.where(beta == 0, own_right, other_right),
        jnp.where(beta == 0, other_right, own_right),
    ])
    packed, right = lax.optimization_barrier((packed, right))
    arrived = lax.all_to_all(packed, everyone, split_axis=0, concat_axis=0, tiled=True)

    left_shape = jax.ShapeDtypeStruct((rows, rank2), f32)
    right_shape = jax.ShapeDtypeStruct((cols, rank2), f32)

    def parts_shape(count, length):
        return jax.ShapeDtypeStruct((count, length // count + TAIL, rank2), f32)

    left_parts = parts_shape(n_pair, rows)
    right_parts = parts_shape(2 * n_src, cols)
    sums_shape = jax.ShapeDtypeStruct((devices, 128), f32)

    def call(kernel, name, out_shape, inputs, **kw):
        return pl.pallas_call(
            kernel,
            out_shape=out_shape,
            in_specs=[pl.BlockSpec(memory_space=pltpu.SMEM)]
            + [pl.BlockSpec(memory_space=pltpu.VMEM)] * inputs,
            compiler_params=params(),
            name=name,
            **kw,
        )

    target, weight, start, parts = call(
        lambda *refs: first_kernel(
            *refs, n_src=n_src, n_rcv=n_rcv, slots=slots, edge=edge,
            per_src=per_src, per_rcv=per_rcv,
        ),
        "first_gradient",
        (
            jax.ShapeDtypeStruct((tiles, rows, width), bf16),
            jax.ShapeDtypeStruct((tiles, mids, width), f32),
            left_shape,
            left_parts,
        ),
        3,
        scratch_shapes=[
            pltpu.VMEM((rows, width), f32), pltpu.VMEM((rows, width), bf16),
            pltpu.VMEM((rows, rank2), f32),
        ],
    )(meta, arrived, left_factor.reshape(mids, 2, edge, rank2), right)

    def send(parts, axis):
        return lax.all_to_all(
            parts.astype(jnp.float16), axis, split_axis=0, concat_axis=0, tiled=True
        )

    def spread(parts, axis):
        summed = pl.pallas_call(
            sum_kernel,
            out_shape=jax.ShapeDtypeStruct(parts.shape, f32),
            compiler_params=params(),
            name="sum_parts",
        )(send(parts, axis).astype(f32))
        return send(summed, axis)

    def shared(message, factor, by_left, copies):
        sums, grad = pl.pallas_call(
            lambda *refs: curve_kernel(*refs, edge=edge, copies=copies, by_left=by_left),
            out_shape=(sums_shape, left_shape if by_left else right_shape),
            compiler_params=params(),
            name="left_curve" if by_left else "right_curve",
        )(message.astype(f32), factor, weight)
        sums = lax.all_to_all(sums, everyone, split_axis=0, concat_axis=0, tiled=True)
        return sums, grad

    def shared_left(parts, factor, *before):
        message = spread(parts, "pair")
        other = lax.ppermute(message, "beta", swap)
        sums, grad = shared(message, factor, True, n_pair)
        sums, *others = lax.optimization_barrier((sums, *before, other))
        return sums, grad, *others

    right_group = ("src", "beta")
    sums, grad, other = shared_left(parts, right)
    left_one, parts_r = call(
        lambda *refs: left_update_kernel(*refs, edge=edge),
        "left_update", (left_shape, right_parts), 6,
        scratch_shapes=[pltpu.VMEM((cols, rank2), f32)],
    )(meta, sums, target, weight, start, grad, right)
    sums_r, grad_r = shared(spread(parts_r, right_group), left_one, False, 2 * n_src)
    right_one, parts = call(
        lambda *refs: right_update_kernel(*refs, edge=edge),
        "right_update", (right_shape, left_parts), 9,
        scratch_shapes=[pltpu.VMEM((rows, rank2), f32)],
    )(meta, sums, sums_r, target, weight, start, grad, right, left_one, grad_r)
    sums_two, grad_two, other, other_two = shared_left(parts, right_one, other)
    in_vmem = pl.BlockSpec(memory_space=pltpu.VMEM)
    left_two, left_out, parts_r = pl.pallas_call(
        lambda *refs: left_again_kernel(*refs, edge=edge),
        out_shape=(
            jax.ShapeDtypeStruct((rows, rank2), bf16),
            jax.ShapeDtypeStruct((mids, 2, edge, rank2), f32),
            right_parts,
        ),
        in_specs=[pl.BlockSpec(memory_space=pltpu.SMEM)] + [in_vmem] * 14
        + [pl.BlockSpec(memory_space=pltpu.HBM)],
        out_specs=(in_vmem, pl.BlockSpec(memory_space=pltpu.HBM), in_vmem),
        scratch_shapes=[pltpu.VMEM((mids, edge, rank2), f32)] * 2
        + [pltpu.VMEM((cols, rank2), f32), pltpu.SemaphoreType.DMA((3,))],
        compiler_params=params(),
        name="left_again",
    )(
        meta, sums, sums_r, sums_two, target, weight, start, grad, right, left_one,
        grad_two, grad_r, right_one, other.astype(f32), other_two.astype(f32),
        left_factor.reshape(mids, 2, edge, rank2),
    )
    sums_r_two, grad_r_two = shared(spread(parts_r, right_group), left_two, False, 2 * n_src)
    right_out = call(
        right_last_kernel, "right_last", jax.ShapeDtypeStruct((own_cols, rank2), f32), 3,
    )(meta, sums_r_two, grad_r_two, right_one)
    return left_out.reshape(left_factor.shape), right_out.reshape(right_factor.shape)


def solution(mesh):
    n_src, n_rcv = mesh.shape["src"], mesh.shape["rcv"]
    split = jax.sharding.Mesh(
        mesh.devices.reshape(n_src, n_rcv // 2, 2), ("src", "pair", "beta")
    )
    rcv = ("pair", "beta")
    return jax.shard_map(
        per_device,
        mesh=split,
        in_specs=(
            P(None, "src", rcv),
            P("src", rcv),
            P(),
            P(None, "src", None, None),
            P(None, rcv, None, None),
        ),
        out_specs=(P(None, "src", None, None), P(None, rcv, None, None)),
        check_vma=False,
    )
```

```python
import jax
import jax.numpy as jnp
from jax import lax
from jax.experimental import pallas as pl
from jax.experimental.pallas import tpu as pltpu
from jax.sharding import PartitionSpec as P

EPSILON = 1e-06
REACH = 8
SLOTS = 8
TAIL = 8
ABSENT = 1024.0
LIMIT = 512.0
VMEM = 24 * 1024 * 1024
f32 = jnp.float32
bf16 = jnp.bfloat16


def params():
    return pltpu.CompilerParams(vmem_limit_bytes=VMEM)


def mod(x, n):
    assert n & (n - 1) == 0
    return x & (n - 1)


def div(x, n):
    assert n & (n - 1) == 0
    return x >> (n.bit_length() - 1)


def nt(a, b):
    return lax.dot_general(a, b, (((1,), (1,)), ((), ())), preferred_element_type=f32)


def nn(a, b):
    return lax.dot_general(a, b, (((1,), (0,)), ((), ())), preferred_element_type=f32)


def tn(a, b):
    return lax.dot_general(a, b, (((0,), (0,)), ((), ())), preferred_element_type=f32)


def stacked(factor, edge):
    half = factor.shape[1] // 2
    rounded = factor.astype(bf16)
    turned = jnp.concatenate([-rounded[:, half:], rounded[:, :half]], axis=1)
    pieces = []
    for t in range(factor.shape[0] // edge):
        rows = slice(t * edge, (t + 1) * edge)
        pieces += [rounded[rows], turned[rows]]
    return jnp.concatenate(pieces, axis=0)


def combined(products, edge):
    half = products.shape[1] // 2
    pieces = []
    for t in range(products.shape[0] // (2 * edge)):
        upper = products[2 * t * edge : (2 * t + 1) * edge]
        lower = products[(2 * t + 1) * edge : (2 * t + 2) * edge]
        pieces.append(jnp.concatenate(
            [upper[:, :half] + lower[:, half:], upper[:, half:] - lower[:, :half]], axis=1
        ))
    return jnp.concatenate(pieces, axis=0)


def step_of(sums):
    lane = lax.broadcasted_iota(jnp.int32, sums.shape, 1)
    numerator = jnp.sum(jnp.where(lane == 0, sums, 0.0), keepdims=True)
    denominator = jnp.sum(jnp.where(lane == 1, sums, 0.0), keepdims=True)
    return numerator / (denominator + EPSILON)


def sums_out(numerator, denominator, shape):
    lane = lax.broadcasted_iota(jnp.int32, shape, 1)
    return jnp.where(lane == 0, numerator, jnp.where(lane == 1, denominator, 0.0))


def weighted(field, weight, edge):
    blocks, columns = weight.shape
    return (field.reshape(blocks, edge, columns) * weight[:, None, :]).reshape(field.shape)


def power(level):
    found = jnp.full_like(level, 2.0 ** (-8 * REACH))
    for k in range(1 - REACH, REACH + 1):
        found = jnp.where(level >= k, 2.0 ** (8 * k), found)
    return found


def steady(values):
    near = values.astype(bf16).astype(f32)
    spread = values * (2.0 ** 13 + 1.0)
    rounded = spread - (spread - values)
    same = rounded.astype(bf16).astype(f32) == near
    return jnp.where(same, values, near + 0.8 * (values - near))


def encode(values, out_ref, last=False):
    count, padded, width = out_ref.shape
    rows = padded - TAIL
    peak = jnp.max(jnp.abs(values), keepdims=True)
    level = jnp.full_like(peak, -REACH)
    for k in range(1 - REACH, REACH + 1):
        level = jnp.where(peak >= 2.0 ** (8 * k + 7), float(k), level)
    scaled = values * power(-level)
    scaled = (steady(scaled) if last else scaled).reshape(-1, rows, width)
    out_ref[:, :rows] = jnp.broadcast_to(scaled, (count, rows, width))
    out_ref[:, rows:] = jnp.broadcast_to(level[None], (count, TAIL, width))


def decode(message_ref):
    rows = message_ref.shape[1] - TAIL
    return message_ref[:, :rows] * power(message_ref[:, rows : rows + 1])


def place(own, other, beta, out_ref):
    rows = own.shape[0]
    out_ref[pl.ds(pl.multiple_of(beta * rows, rows), rows), :] = own
    out_ref[pl.ds(pl.multiple_of((1 - beta) * rows, rows), rows), :] = other


def pack_kernel(meta_ref, flags_ref, data_ref, out_ref, buf_ref, sem_ref, *, n_src, n_rcv):
    _, groups, _, edge, width = data_ref.shape
    copies = [
        pltpu.make_async_copy(
            data_ref.at[:, :, sigma], buf_ref.at[sigma % SLOTS], sem_ref.at[sigma % SLOTS]
        )
        for sigma in range(n_src)
    ]
    for copy in copies[:SLOTS]:
        copy.start()
    pairs = width // (2 * edge)
    odd = mod(meta_ref[1], 2)
    placed = (odd, 1 - odd)
    for sigma in range(n_src):
        copies[sigma].wait()
        for u in range(groups):
            for pair in range(pairs):
                re = buf_ref[sigma % SLOTS, 0, u, :, pair * 2 * edge : (pair + 1) * 2 * edge]
                im = buf_ref[sigma % SLOTS, 1, u, :, pair * 2 * edge : (pair + 1) * 2 * edge]
                first = jnp.concatenate([re[:, :edge], im[:, :edge]], axis=1)
                second = jnp.concatenate([re[:, edge:], im[:, edge:]], axis=1)
                for side, block in ((0, first), (1, second)):
                    column = 2 * pair + side
                    source = sigma + n_src * u
                    seen = flags_ref[source, column] != 0
                    diff = (column - source) % n_rcv
                    q = diff // 2
                    turns = (source + diff) // n_rcv + (sigma + q) // n_src
                    near = (sigma + diff) % n_rcv < n_rcv // 2
                    slot = 2 * (diff % 2) + (u // 2 if near else u % 2)
                    dest = (sigma + q) % n_src * n_rcv + 2 * q + placed[(u + turns) % 2]
                    out_ref[dest, slot] = jnp.where(
                        seen, block, jnp.full_like(block, ABSENT)
                    )
        if sigma + SLOTS < n_src:
            copies[sigma + SLOTS].start()


def first_kernel(meta_ref, blocks_ref, left_ref, own_ref, other_ref,
                 target_ref, w_ref, start_ref, right_ref, out_ref, product_ref, residual_ref, grad_ref,
                 *, n_src, n_rcv, slots, edge, per_src, per_rcv):
    src, pair, beta, band = meta_ref[0], meta_ref[2], meta_ref[3], meta_ref[4]
    total = n_src * per_src
    mids = left_ref.shape[0]
    groups = per_src // n_src
    half = n_rcv // 2
    tiles = target_ref.shape[0]
    width = 2 * edge
    per_tile = target_ref.shape[2] // width
    start_ref[...] = left_ref[:, pl.ds(beta, 1)].reshape(start_ref.shape)
    place(own_ref[...], other_ref[...], beta, right_ref)
    left_b = start_ref[...].astype(bf16)
    for tile in range(tiles):
        rows = slice(tile * per_tile * edge, (tile + 1) * per_tile * edge)
        stack = stacked(right_ref[rows, :], edge)
        product_ref[...] = nt(left_b, stack)
        for side in range(per_tile):
            column = tile * per_tile + side
            tau, t = column // slots, column % slots
            residue = 2 * pair + tau
            offset = n_rcv * t + residue - half * slots
            inside = jnp.abs(offset) <= band
            cols = slice(side * width, (side + 1) * width)
            for mm in range(mids):
                mid = src + n_src * (2 * mm + beta)
                source = mod(mid - (offset >> 1), total)
                receiver = mod(source + offset, total)
                u = div(mod(source, per_src), n_src)
                near = mod(mod(source, n_src) + residue, n_rcv) < half
                slot = 2 * tau + jnp.where(near, div(u, 2), mod(u, 2))
                message = div(source, per_src) * n_rcv + div(receiver, per_rcv)
                wide = blocks_ref[message, slot].astype(f32)
                keep = jnp.logical_and(wide < LIMIT, inside)
                at = slice(mm * edge, (mm + 1) * edge)
                target_ref[tile, at, cols] = jnp.where(keep, wide, 0.0).astype(bf16)
                w_ref[tile, mm : mm + 1, cols] = jnp.where(keep[0:1], 1.0, 0.0)
                residual_ref[at, cols] = jnp.where(
                    keep, product_ref[at, cols] - wide, 0.0
                ).astype(bf16)
        grad = nn(residual_ref[...], stack)
        grad_ref[...] = grad if tile == 0 else grad_ref[...] + grad
    encode(grad_ref[...], out_ref)


def sum_kernel(parts_ref, out_ref):
    encode(jnp.sum(decode(parts_ref), axis=0), out_ref, last=True)


def curve_kernel(message_ref, factor_ref, w_ref, out_ref, grad_ref, *, edge, copies, by_left):
    grad_ref[...] = decode(message_ref).reshape(grad_ref.shape)
    left_ref, right_ref = (grad_ref, factor_ref) if by_left else (factor_ref, grad_ref)
    left_b = left_ref[...].astype(bf16)
    mids = left_b.shape[0] // edge
    tiles, _, width = w_ref.shape
    total = jnp.zeros((mids, width), f32)
    for tile in range(tiles):
        curve = nt(left_b, stacked(tile_rows(right_ref, tile, w_ref), edge))
        squares = (curve * curve).reshape(mids, edge, width)
        total = total + jnp.sum(squares, axis=1) * w_ref[tile]
    grad = grad_ref[...]
    numerator = jnp.sum(grad * grad, keepdims=True) * (1.0 / copies)
    out_ref[...] = sums_out(numerator, jnp.sum(total, keepdims=True), out_ref.shape)


def residual_of(target, weight, lefts, stacks, steps, edge):
    residual = nt(lefts[0], stacks[0]) - target.astype(f32)
    for left, stack, step in zip(lefts[1:], stacks[1:], steps):
        residual = residual - step * nt(left, stack)
    return weighted(residual, weight, edge).astype(bf16)


def tile_rows(ref, tile, w_ref):
    rows = w_ref.shape[2] // 2
    return ref[tile * rows : (tile + 1) * rows, :]


def left_update_kernel(meta_ref, sums_ref, target_ref, w_ref, start_ref, first_grad_ref,
                       right_ref, left_out_ref, out_ref, parts_ref, *, edge):
    step = step_of(sums_ref[...])
    start = start_ref[...]
    grad = first_grad_ref[...]
    new = start - step * grad
    left_out_ref[...] = new
    lefts = [start.astype(bf16), grad.astype(bf16)]
    new_b = new.astype(bf16)
    rows = w_ref.shape[2] // 2
    for tile in range(w_ref.shape[0]):
        stack = stacked(tile_rows(right_ref, tile, w_ref), edge)
        residual = residual_of(
            target_ref[tile], w_ref[tile], lefts, [stack, stack], [step], edge
        )
        parts_ref[tile * rows : (tile + 1) * rows, :] = combined(tn(new_b, residual).T, edge)
    encode(parts_ref[...], out_ref)


def left_again_kernel(meta_ref, sums_ref, sums_r_ref, sums_now_ref, target_ref, w_ref, start_ref,
                      first_grad_ref, right_ref, left_ref, grad_ref, grad_r_ref, right_now_ref,
                      *refs, edge):
    (first_ref, second_ref, given_ref, left_b_ref, left_out_ref, out_ref,
     own_ref, other_ref, parts_ref, sem_ref) = refs
    beta = meta_ref[3]
    fetch = pltpu.make_async_copy(given_ref.at[:, 1 - beta], other_ref, sem_ref.at[0])
    own_out = pltpu.make_async_copy(own_ref, left_out_ref.at[:, beta], sem_ref.at[1])
    other_out = pltpu.make_async_copy(other_ref, left_out_ref.at[:, 1 - beta], sem_ref.at[2])
    fetch.start()
    steps = [step_of(ref[...]) for ref in (sums_ref, sums_r_ref, sums_now_ref)]
    new = left_ref[...] - steps[2] * grad_ref[...]
    own_ref[...] = new.reshape(own_ref.shape)
    own_out.start()
    new_b = new.astype(bf16)
    left_b_ref[...] = new_b
    lefts = [ref[...].astype(bf16) for ref in (start_ref, first_grad_ref, left_ref, grad_ref)]
    rows = w_ref.shape[2] // 2
    for tile in range(w_ref.shape[0]):
        stack, stack_r, stack_now = [
            stacked(tile_rows(ref, tile, w_ref), edge)
            for ref in (right_ref, grad_r_ref, right_now_ref)
        ]
        if tile == 1:
            fetch.wait()
            taken = other_ref[...].reshape(left_ref.shape)
            for step, ref in ((steps[0], first_ref), (steps[2], second_ref)):
                taken = taken - step * decode(ref).reshape(taken.shape)
            other_ref[...] = taken.reshape(other_ref.shape)
            other_out.start()
        residual = residual_of(
            target_ref[tile], w_ref[tile], lefts, [stack, stack, stack_r, stack_now], steps, edge
        )
        parts_ref[tile * rows : (tile + 1) * rows, :] = combined(tn(new_b, residual).T, edge)
    encode(parts_ref[...], out_ref)
    own_out.wait()
    other_out.wait()


def right_update_kernel(meta_ref, sums_ref, sums_r_ref, target_ref, w_ref, start_ref,
                        first_grad_ref, right_ref, left_ref, grad_r_ref, own_ref, other_ref,
                        right_out_ref, out_ref, grad_ref, *, edge):
    step = step_of(sums_ref[...])
    step_r = step_of(sums_r_ref[...])
    place(own_ref[...], other_ref[...], meta_ref[3], right_out_ref)
    right_out_ref[...] = right_out_ref[...] - step_r * grad_r_ref[...]
    start = start_ref[...]
    lefts = [value.astype(bf16) for value in (start, first_grad_ref[...], left_ref[...])]
    for tile in range(w_ref.shape[0]):
        stack, stack_r, stack_now = [
            stacked(tile_rows(ref, tile, w_ref), edge)
            for ref in (right_ref, grad_r_ref, right_out_ref)
        ]
        residual = residual_of(
            target_ref[tile], w_ref[tile], lefts, [stack, stack, stack_r], [step, step_r], edge
        )
        grad = nn(residual, stack_now)
        grad_ref[...] = grad if tile == 0 else grad_ref[...] + grad
    encode(grad_ref[...], out_ref)


def right_last_kernel(meta_ref, sums_ref, grad_r_ref, right_ref, right_out_ref):
    own = right_out_ref.shape[0]
    rows = pl.ds(pl.multiple_of(meta_ref[3] * own, own), own)
    right_out_ref[...] = right_ref[rows, :] - step_of(sums_ref[...]) * grad_r_ref[rows, :]


def per_device(data, observed, band_width, left_factor, right_factor):
    n_src = lax.axis_size("src")
    n_pair = lax.axis_size("pair")
    n_rcv = 2 * n_pair
    devices = n_src * n_rcv
    per_src, per_rcv = observed.shape
    edge = data.shape[1] // per_src
    groups = per_src // n_src
    slots = right_factor.shape[0]
    rank2 = left_factor.shape[3]
    mids = per_src // 2
    rows = mids * edge
    own_cols = slots * edge
    cols = 2 * own_cols
    width = 4 * edge
    tiles = 2 * cols // width
    everyone = ("src", "pair", "beta")
    swap = [(0, 1), (1, 0)]

    src = lax.axis_index("src")
    pair = lax.axis_index("pair")
    beta = lax.axis_index("beta")
    meta = jnp.stack([src, 2 * pair + beta, pair, beta, band_width[0]]).astype(jnp.int32)

    own_right = right_factor.reshape(own_cols, rank2)
    own_short = own_right.astype(bf16)
    other_short = lax.ppermute(own_short, "beta", swap)
    packed = pl.pallas_call(
        lambda *refs: pack_kernel(*refs, n_src=n_src, n_rcv=n_rcv),
        out_shape=jax.ShapeDtypeStruct((devices, groups, edge, 2 * edge), bf16),
        in_specs=[pl.BlockSpec(memory_space=pltpu.SMEM)] * 2
        + [pl.BlockSpec(memory_space=pltpu.HBM)],
        out_specs=pl.BlockSpec(memory_space=pltpu.VMEM),
        scratch_shapes=[
            pltpu.VMEM((SLOTS, 2, groups, edge, data.shape[2]), bf16),
            pltpu.SemaphoreType.DMA((SLOTS,)),
        ],
        compiler_params=params(),
        name="pack",
    )(meta, observed, pltpu.with_memory_space_constraint(
        data.reshape(2, groups, n_src, edge, data.shape[2]), pltpu.HBM
    ))
    packed, other_short = lax.optimization_barrier((packed, other_short))
    arrived = lax.all_to_all(packed, everyone, split_axis=0, concat_axis=0, tiled=True)

    left_shape = jax.ShapeDtypeStruct((rows, rank2), f32)
    right_shape = jax.ShapeDtypeStruct((cols, rank2), f32)

    def parts_shape(count, length):
        return jax.ShapeDtypeStruct((count, length // count + TAIL, rank2), f32)

    left_parts = parts_shape(n_pair, rows)
    right_parts = parts_shape(2 * n_src, cols)
    sums_shape = jax.ShapeDtypeStruct((devices, 128), f32)

    def call(kernel, name, out_shape, inputs, **kw):
        return pl.pallas_call(
            kernel,
            out_shape=out_shape,
            in_specs=[pl.BlockSpec(memory_space=pltpu.SMEM)]
            + [pl.BlockSpec(memory_space=pltpu.VMEM)] * inputs,
            compiler_params=params(),
            name=name,
            **kw,
        )

    target, weight, start, right, parts = call(
        lambda *refs: first_kernel(
            *refs, n_src=n_src, n_rcv=n_rcv, slots=slots, edge=edge,
            per_src=per_src, per_rcv=per_rcv,
        ),
        "first_gradient",
        (
            jax.ShapeDtypeStruct((tiles, rows, width), bf16),
            jax.ShapeDtypeStruct((tiles, mids, width), f32),
            left_shape,
            jax.ShapeDtypeStruct((cols, rank2), bf16),
            left_parts,
        ),
        4,
        scratch_shapes=[
            pltpu.VMEM((rows, width), f32), pltpu.VMEM((rows, width), bf16),
            pltpu.VMEM((rows, rank2), f32),
        ],
    )(meta, arrived, left_factor.reshape(mids, 2, edge, rank2), own_short, other_short)

    def send(parts, axis):
        return lax.all_to_all(
            parts.astype(jnp.float16), axis, split_axis=0, concat_axis=0, tiled=True
        )

    def spread(parts, axis):
        summed = pl.pallas_call(
            sum_kernel,
            out_shape=jax.ShapeDtypeStruct(parts.shape, f32),
            compiler_params=params(),
            name="sum_parts",
        )(send(parts, axis).astype(f32))
        return send(summed, axis)

    def shared(message, factor, by_left, copies):
        sums, grad = pl.pallas_call(
            lambda *refs: curve_kernel(*refs, edge=edge, copies=copies, by_left=by_left),
            out_shape=(sums_shape, left_shape if by_left else right_shape),
            compiler_params=params(),
            name="left_curve" if by_left else "right_curve",
        )(message.astype(f32), factor, weight)
        sums = lax.all_to_all(sums, everyone, split_axis=0, concat_axis=0, tiled=True)
        return sums, grad

    def shared_left(parts, factor, *before):
        message = spread(parts, "pair")
        other = lax.ppermute(message, "beta", swap)
        sums, grad = shared(message, factor, True, n_pair)
        sums, *others = lax.optimization_barrier((sums, *before, other))
        return sums, grad, *others

    right_group = ("src", "beta")
    sums, grad, other = shared_left(parts, right)
    left_one, parts_r = call(
        lambda *refs: left_update_kernel(*refs, edge=edge),
        "left_update", (left_shape, right_parts), 6,
        scratch_shapes=[pltpu.VMEM((cols, rank2), f32)],
    )(meta, sums, target, weight, start, grad, right)
    message = spread(parts_r, right_group)
    message, own_right = lax.optimization_barrier((message, own_right))
    other_right = lax.ppermute(own_right, "beta", swap)
    sums_r, grad_r = shared(message, left_one, False, 2 * n_src)
    sums_r, other_right = lax.optimization_barrier((sums_r, other_right))
    right_one, parts = call(
        lambda *refs: right_update_kernel(*refs, edge=edge),
        "right_update", (right_shape, left_parts), 11,
        scratch_shapes=[pltpu.VMEM((rows, rank2), f32)],
    )(
        meta, sums, sums_r, target, weight, start, grad, right, left_one, grad_r,
        own_right, other_right,
    )
    sums_two, grad_two, other, other_two = shared_left(parts, right_one, other)
    in_vmem = pl.BlockSpec(memory_space=pltpu.VMEM)
    left_two, left_out, parts_r = pl.pallas_call(
        lambda *refs: left_again_kernel(*refs, edge=edge),
        out_shape=(
            jax.ShapeDtypeStruct((rows, rank2), bf16),
            jax.ShapeDtypeStruct((mids, 2, edge, rank2), f32),
            right_parts,
        ),
        in_specs=[pl.BlockSpec(memory_space=pltpu.SMEM)] + [in_vmem] * 14
        + [pl.BlockSpec(memory_space=pltpu.HBM)],
        out_specs=(in_vmem, pl.BlockSpec(memory_space=pltpu.HBM), in_vmem),
        scratch_shapes=[pltpu.VMEM((mids, edge, rank2), f32)] * 2
        + [pltpu.VMEM((cols, rank2), f32), pltpu.SemaphoreType.DMA((3,))],
        compiler_params=params(),
        name="left_again",
    )(
        meta, sums, sums_r, sums_two, target, weight, start, grad, right, left_one,
        grad_two, grad_r, right_one, other.astype(f32), other_two.astype(f32),
        left_factor.reshape(mids, 2, edge, rank2),
    )
    sums_r_two, grad_r_two = shared(spread(parts_r, right_group), left_two, False, 2 * n_src)
    right_out = call(
        right_last_kernel, "right_last", jax.ShapeDtypeStruct((own_cols, rank2), f32), 3,
    )(meta, sums_r_two, grad_r_two, right_one)
    return left_out.reshape(left_factor.shape), right_out.reshape(right_factor.shape)


def solution(mesh):
    n_src, n_rcv = mesh.shape["src"], mesh.shape["rcv"]
    split = jax.sharding.Mesh(
        mesh.devices.reshape(n_src, n_rcv // 2, 2), ("src", "pair", "beta")
    )
    rcv = ("pair", "beta")
    return jax.shard_map(
        per_device,
        mesh=split,
        in_specs=(
            P(None, "src", rcv),
            P("src", rcv),
            P(),
            P(None, "src", None, None),
            P(None, rcv, None, None),
        ),
        out_specs=(P(None, "src", None, None), P(None, rcv, None, None)),
        check_vma=False,
    )
```
